256 devices in a mesh: leaf: 32 (over z, y), head: 8 (over x, core).
Axes of the slice: x: 4, y: 4, z: 8, core: 2. Of those that a mesh axis runs over, the one named last changes fastest.
Arguments:
- query_in: bfloat16 [4096, 8192], P('leaf', 'head'), may hold values from -12 to 12
- key_in: bfloat16 [4096, 1024], P(('leaf', 'head')), may hold values from -12 to 12
- value_in: bfloat16 [4096, 1024], P(('leaf', 'head')), may hold values from -6 to 6
- out_grad: bfloat16 [4096, 8192], P('leaf', 'head'), may hold values from -6 to 6
- ancestry: int32 [32, 8], replicated, may hold values from -1 to 31, as said below
- node_len: int32 [32], replicated, may hold values from 64 to 128, as said below
Outputs:
- attended: bfloat16 [4096, 8192], P('leaf', 'head')
- query_grad: float32 [4096, 8192], P('leaf', 'head')
- key_grad: float32 [4096, 1024], P(('leaf', 'head'))
- value_grad: float32 [4096, 1024], P(('leaf', 'head'))
The draws below stay inside these ranges and needn't reach their ends.
Inputs may be any that keep to these rules, and one draw needn't show every extreme that they name: `ancestry`: row g lists the ancestors of node g from the root, node 0, at column 0 down to node g itself at column depth(g), then -1; every ancestor of a node comes before it; nodes 0 to 3 form a chain. `node_len`: the root's length is 128, the last node's 128 // 2.
All inputs are finite; a program needn't handle non-finite values.
Results may differ from the reference program's by a relative error of at most 0.019.
Values may be sent and summed in bfloat16 or wider, within the bound.
No kernel may reach another device: no remote copies, remote signals or barrier semaphores. Data moves between devices by JAX's collectives and lax.ppermute only.
A program may use at most 64 MiB of HBM per device.

```python
import jax
import jax.numpy as jnp
from jax import lax

QH = 64
KVH = 8
HD = 128
BLK = 128
ANC = 8
TOKENS = 4096
NODES = 32


def draw_query_in(key, part):
    values = jnp.clip(jax.random.normal(jax.random.fold_in(key, 1), (TOKENS, QH * HD), jnp.float32), -6.0, 6.0)
    return values.astype(jnp.bfloat16)


def draw_key_in(key, part):
    values = jnp.clip(jax.random.normal(jax.random.fold_in(key, 3), (TOKENS, KVH * HD), jnp.float32), -6.0, 6.0)
    return values.astype(jnp.bfloat16)


def draw_ancestry(key, part):
    picks = jax.random.randint(jax.random.fold_in(key, 5), (NODES,), 0, 1 << 20)
    level = jnp.arange(ANC, dtype=jnp.int32)

    def step(carry, item):
        previous, stack = carry
        node, pick = item
        deeper = 1 + pick % jnp.minimum(previous + 1, ANC - 1)
        depth = jnp.where(node < ANC // 2, node, deeper).astype(jnp.int32)
        stack = jnp.where(level == depth, node, stack)
        row = jnp.where(level <= depth, stack, -1).astype(jnp.int32)
        return ((depth, stack), row)
    start = (jnp.int32(0), jnp.full((ANC,), -1, jnp.int32))
    _, rows = lax.scan(step, start, (jnp.arange(NODES, dtype=jnp.int32), picks))
    return rows


def draw_node_len(key, part):
    lengths = jax.random.randint(jax.random.fold_in(key, 6), (NODES,), BLK // 2, BLK + 1)
    nodes = jnp.arange(NODES, dtype=jnp.int32)
    lengths = jnp.where(nodes == 0, BLK, lengths)
    lengths = jnp.where(nodes == NODES - 1, BLK // 2, lengths)
    return lengths.astype(jnp.int32)


def block_levels(key, dims, pieces, smallest, high):
    def one(dim, parts):
        heights = jax.random.uniform(jax.random.fold_in(jax.random.fold_in(key, 6), dim), (parts,), jnp.float32, smallest / len(pieces), high / len(pieces))
        return jnp.repeat(jnp.exp(heights), dims[dim] // parts).reshape((-1,) + (1,) * (len(dims) - dim - 1))

    loudness = one(*pieces[0])
    for cut in pieces[1:]:
        loudness = loudness * one(*cut)
    return loudness


def noise(own_key, shape, width, bound, shards=(), held_as=jnp.bfloat16):
    factor_of = block_levels(own_key, shape, shards, -0.22, 0.18) if shards else 1.0
    entries = jax.random.normal(own_key, shape, jnp.float32) * width * factor_of
    return jnp.minimum(jnp.maximum(entries, -bound), bound).astype(held_as)


def setup_inputs(seed: int = 0) -> dict:
    arg_keys = jax.random.split(jax.random.key(seed), 7)
    return {
        "query_in": draw_query_in(jax.random.fold_in(arg_keys[6], 71), 0),
        "key_in": draw_key_in(jax.random.fold_in(arg_keys[6], 71), 0),
        "value_in": noise(arg_keys[2], (TOKENS, KVH * HD), 1.0, 6.0, ((0, 256),)),
        "out_grad": noise(arg_keys[3], (TOKENS, QH * HD), 1.0, 6.0, ((0, 32), (1, 8))),
        "ancestry": draw_ancestry(jax.random.fold_in(arg_keys[6], 71), 0),
        "node_len": draw_node_len(jax.random.fold_in(arg_keys[6], 71), 0),
    }


def reference(query_in, key_in, value_in, out_grad, ancestry, node_len):
    scale = HD ** -0.5
    group = QH // KVH
    position = jnp.arange(TOKENS, dtype=jnp.int32)
    lengths = jnp.repeat(node_len, BLK)
    tags = jnp.where(position % BLK < lengths, position // BLK, -2).astype(jnp.int32)
    ancestor_rows = jnp.repeat(ancestry, BLK, axis=0).reshape(NODES, BLK, ANC)
    query_heads = query_in.reshape(NODES, BLK, KVH, group, HD).transpose(2, 0, 1, 3, 4)
    grad_heads = out_grad.reshape(NODES, BLK, KVH, group, HD).transpose(2, 0, 1, 3, 4)
    key_heads = key_in.reshape(TOKENS, KVH, HD).transpose(1, 0, 2)
    value_heads = value_in.reshape(TOKENS, KVH, HD).transpose(1, 0, 2)
    query_position = position.reshape(NODES, BLK)

    def one_head(items):
        query_h, grad_h, key_h, value_h = items
        key_wide = key_h.astype(jnp.float32)
        value_wide = value_h.astype(jnp.float32)

        def block(carry, blocks):
            key_acc, value_acc = carry
            query_b, grad_b, query_pos, ancestor_b = blocks
            query_wide = query_b.astype(jnp.float32)
            grad_wide = grad_b.astype(jnp.float32)
            member = jnp.any(ancestor_b[:, :, None] == tags[None, None, :], axis=1)
            own_node = query_pos // BLK
            allowed = member & ((tags[None, :] != own_node[:, None]) | (position[None, :] <= query_pos[:, None]))
            logits = jnp.einsum("rgd,cd->grc", query_wide, key_wide) * scale
            logits = jnp.where(allowed[None], logits, -jnp.inf)
            row_top = jnp.max(logits, axis=-1)
            expo = jnp.exp(logits - row_top[..., None])
            total = jnp.sum(expo, axis=-1)
            lse = row_top + jnp.log(total)
            expo_low = lax.optimization_barrier(expo.astype(jnp.bfloat16)).astype(jnp.float32)
            output = (jnp.einsum("grc,cd->grd", expo_low, value_wide) / total[..., None]).astype(jnp.bfloat16)
            delta = jnp.sum(grad_wide.transpose(1, 0, 2) * output.astype(jnp.float32), axis=-1)
            weights = jnp.exp(logits - lse[..., None])
            probs = lax.optimization_barrier(weights.astype(jnp.bfloat16)).astype(jnp.float32)
            dprob = jnp.einsum("rgd,cd->grc", grad_wide, value_wide)
            dlogit = lax.optimization_barrier((weights * (dprob - delta[..., None])).astype(jnp.bfloat16)).astype(jnp.float32)
            query_g = scale * jnp.einsum("grc,cd->rgd", dlogit, key_wide)
            key_acc = key_acc + scale * jnp.einsum("grc,rgd->cd", dlogit, query_wide)
            value_acc = value_acc + jnp.einsum("grc,rgd->cd", probs, grad_wide)
            return (key_acc, value_acc), (output, query_g)

        start = (jnp.zeros((TOKENS, HD), jnp.float32), jnp.zeros((TOKENS, HD), jnp.float32))
        (key_acc, value_acc), (outputs, query_gs) = lax.scan(block, start, (query_h, grad_h, query_position, ancestor_rows))
        return outputs, query_gs, key_acc, value_acc

    outputs, query_gs, key_gs, value_gs = lax.map(one_head, (query_heads, grad_heads, key_heads, value_heads))
    attended = outputs.transpose(1, 3, 0, 2, 4).reshape(TOKENS, QH * HD)
    query_grad = query_gs.transpose(1, 2, 0, 3, 4).reshape(TOKENS, QH * HD)
    key_grad = key_gs.transpose(1, 0, 2).reshape(TOKENS, KVH * HD)
    value_grad = value_gs.transpose(1, 0, 2).reshape(TOKENS, KVH * HD)
    return attended, query_grad, key_grad, value_grad
```

```python
import functools

import jax
import jax.numpy as jnp
from jax import lax
from jax.experimental import pallas as pl
from jax.experimental.pallas import tpu as pltpu
from jax.sharding import PartitionSpec as P

QH = 64
KVH = 8
HD = 128
BLK = 128
ANC = 8
NODES = 32
GROUP = QH // KVH
KEYS = ANC * BLK
PAIR = 2
CHUNK = 256
LOG2E = 1.4426950408889634
SCALE = HD ** (-0.5)
FAR = -1e30

NT = (((1,), (1,)), ((), ()))
NN = (((1,), (0,)), ((), ()))


def dot(a, b, dims=NN):
    return lax.dot_general(a, b, dims, preferred_element_type=jnp.float32)


def pick_kernel(anc_ref, rows_ref, out_ref):
    anc = anc_ref[...].reshape(NODES, 1, ANC, 128)
    head = lax.broadcasted_iota(jnp.int32, (NODES, KVH, ANC, 128), 1)
    want = (jnp.broadcast_to(anc, (NODES, KVH, ANC, 128)) * KVH + head).reshape(NODES * KVH * ANC, 128)
    lane = lax.broadcasted_iota(jnp.int32, (NODES * KVH * ANC, 128), 1)
    total = jnp.zeros((NODES * KVH * ANC, HD), jnp.float32)
    halves = []
    for part in range(2):
        halves.append(jnp.where(want == lane + part * 128, 1.0, 0.0).astype(jnp.bfloat16))
    onehot = jnp.concatenate(halves, axis=1)
    out_ref[...] = dot(onehot, rows_ref[...]).astype(jnp.bfloat16)


def add_kernel(code_ref, terms_ref, out_ref):
    row = lax.broadcasted_iota(jnp.int32, (NODES * KVH, NODES * KVH * ANC), 0)
    onehot = jnp.where(code_ref[...] == row, 1.0, 0.0).astype(jnp.bfloat16)
    out_ref[...] = dot(onehot, terms_ref[...]).astype(jnp.bfloat16)


def attention_kernel(
    leaf_ref, anc_ref, len_ref, q_ref, g_ref, kv_ref, out_ref, qg_ref, kvg_ref,
    k_ref, v_ref, kt_ref, vt_ref, e_ref, p_ref, dl_ref, qa_ref, ga_ref,
):
    step = pl.program_id(0)
    leaf = leaf_ref[0]
    wide = PAIR * BLK

    @pl.when(step == 0)
    def _():
        for rr in range(16):
            k_ref[pl.ds(rr * 64, 64), :] = kv_ref[pl.ds(rr * 128, 64), :]
            v_ref[pl.ds(rr * 64, 64), :] = kv_ref[pl.ds(rr * 128 + 64, 64), :]
        kt_ref[...] = k_ref[...].T
        vt_ref[...] = v_ref[...].T

    slot = lax.broadcasted_iota(jnp.int32, (ANC, wide), 0)
    query = lax.broadcasted_iota(jnp.int32, (ANC, wide), 1) % BLK
    limit = jnp.zeros((ANC, wide), jnp.int32)
    for s in range(ANC):
        node = anc_ref[leaf, s]
        length = jnp.where(node >= 0, len_ref[jnp.maximum(node, 0)], 0)
        own = jnp.where(node == leaf, 1, 0)
        here = jnp.where(own == 1, jnp.minimum(query + 1, length), length)
        limit = jnp.where(slot == s, here, limit)

    q2 = jnp.concatenate([q_ref[:, :HD], q_ref[:, HD:]], axis=0)
    g2 = jnp.concatenate([g_ref[:, :HD], g_ref[:, HD:]], axis=0)
    qa_ref[pl.ds(step * wide, wide), :] = q2
    ga_ref[pl.ds(step * wide, wide), :] = g2
    groups = CHUNK // ANC
    tall = jnp.broadcast_to(limit[None], (groups, ANC, wide))
    index = lax.broadcasted_iota(jnp.int32, (groups, ANC, wide), 0)

    top = jnp.full((ANC, wide), FAR, jnp.float32)
    for c in range(KEYS // CHUNK):
        raw = dot(k_ref[pl.ds(c * CHUNK, CHUNK), :], q2, NT) * (SCALE * LOG2E)
        number = index + c * groups
        place = (number % 8) * 16 + number // 8
        masked = jnp.where(place < tall, raw.reshape(groups, ANC, wide), FAR)
        top = jnp.maximum(top, jnp.max(masked, axis=0))
        e_ref[pl.ds(c * CHUNK, CHUNK), :] = masked.reshape(CHUNK, wide)
    row_top = jnp.max(top, axis=0, keepdims=True)
    part = jnp.zeros((ANC, wide), jnp.float32)
    acc = jnp.zeros((HD, wide), jnp.float32)
    for c in range(KEYS // CHUNK):
        expo = jnp.exp2(e_ref[pl.ds(c * CHUNK, CHUNK), :] - row_top)
        e_ref[pl.ds(c * CHUNK, CHUNK), :] = expo
        part = part + jnp.sum(expo.reshape(groups, ANC, wide), axis=0)
        acc = acc + dot(vt_ref[:, pl.ds(c * CHUNK, CHUNK)], expo.astype(jnp.bfloat16))
    total = jnp.sum(part, axis=0, keepdims=True)
    inverse = 1.0 / total
    out_t = (acc * inverse).astype(jnp.bfloat16)
    gt = g2.T
    delta = jnp.sum(gt.astype(jnp.float32) * out_t.astype(jnp.float32), axis=0, keepdims=True)
    for i in range(PAIR):
        out_ref[:, pl.ds(i * HD, HD)] = out_t[:, i * BLK : (i + 1) * BLK].T
    qacc = jnp.zeros((HD, wide), jnp.float32)
    for c in range(KEYS // CHUNK):
        dprob = dot(v_ref[pl.ds(c * CHUNK, CHUNK), :], g2, NT)
        weights = e_ref[pl.ds(c * CHUNK, CHUNK), :] * inverse
        dlogit = (weights * (dprob - delta)).astype(jnp.bfloat16)
        p_ref[step, pl.ds(c * CHUNK, CHUNK), :] = weights.astype(jnp.bfloat16)
        dl_ref[step, pl.ds(c * CHUNK, CHUNK), :] = dlogit
        qacc = qacc + dot(kt_ref[:, pl.ds(c * CHUNK, CHUNK)], dlogit)
    qacc = qacc * SCALE
    for i in range(PAIR):
        qg_ref[:, pl.ds(i * HD, HD)] = qacc[:, i * BLK : (i + 1) * BLK].T

    @pl.when(step == pl.num_programs(0) - 1)
    def _():
        for c in range(KEYS // CHUNK):
            kg = jnp.zeros((CHUNK, HD), jnp.float32)
            vg = jnp.zeros((CHUNK, HD), jnp.float32)
            for b in range(GROUP // PAIR):
                kg = kg + dot(dl_ref[b, pl.ds(c * CHUNK, CHUNK), :], qa_ref[pl.ds(b * wide, wide), :])
                vg = vg + dot(p_ref[b, pl.ds(c * CHUNK, CHUNK), :], ga_ref[pl.ds(b * wide, wide), :])
            kg = (kg * SCALE).astype(jnp.bfloat16)
            vg = vg.astype(jnp.bfloat16)
            for r in range(CHUNK // 64):
                rr = c * (CHUNK // 64) + r
                kvg_ref[pl.ds(rr * 128, 64), :] = kg[r * 64 : (r + 1) * 64]
                kvg_ref[pl.ds(rr * 128 + 64, 64), :] = vg[r * 64 : (r + 1) * 64]


def attend(leaf, ancestry, node_len, query, grad, kv):
    wide = PAIR * HD
    whole = lambda shape: pl.BlockSpec(shape, lambda i, *_: (0,) * len(shape))
    pair = lambda: pl.BlockSpec((BLK, wide), lambda i, *_: (0, i))
    steps = GROUP // PAIR
    return pl.pallas_call(
        attention_kernel,
        out_shape=(
            jax.ShapeDtypeStruct((BLK, GROUP * HD), jnp.bfloat16),
            jax.ShapeDtypeStruct((BLK, GROUP * HD), jnp.float32),
            jax.ShapeDtypeStruct((2 * KEYS, HD), jnp.bfloat16),
        ),
        grid_spec=pltpu.PrefetchScalarGridSpec(
            num_scalar_prefetch=3,
            grid=(steps,),
            in_specs=[pair(), pair(), whole((2 * KEYS, HD))],
            out_specs=[pair(), pair(), whole((2 * KEYS, HD))],
            scratch_shapes=[
                pltpu.VMEM((KEYS, HD), jnp.bfloat16),
                pltpu.VMEM((KEYS, HD), jnp.bfloat16),
                pltpu.VMEM((HD, KEYS), jnp.bfloat16),
                pltpu.VMEM((HD, KEYS), jnp.bfloat16),
                pltpu.VMEM((KEYS, PAIR * BLK), jnp.float32),
                pltpu.VMEM((steps, KEYS, PAIR * BLK), jnp.bfloat16),
                pltpu.VMEM((steps, KEYS, PAIR * BLK), jnp.bfloat16),
                pltpu.VMEM((GROUP * BLK, HD), jnp.bfloat16),
                pltpu.VMEM((GROUP * BLK, HD), jnp.bfloat16),
            ],
        ),
        compiler_params=pltpu.CompilerParams(dimension_semantics=("arbitrary",)),
        name="attend",
    )(leaf, ancestry, node_len, query, grad, kv)


def per_device(query_in, key_in, value_in, out_grad, ancestry, node_len):
    leaf = lax.axis_index("leaf").astype(jnp.int32).reshape(1)
    rows = key_in.shape[0]
    pieces = jnp.stack([key_in.reshape(rows, KVH, HD), value_in.reshape(rows, KVH, HD)], axis=1)
    pieces = pieces.reshape(2 * rows, KVH, HD)
    gathered = lax.all_to_all(pieces, "leaf", split_axis=0, concat_axis=0, tiled=True)
    wide_anc = jnp.broadcast_to(ancestry.reshape(NODES * ANC, 1), (NODES * ANC, 128))
    count = NODES * KVH * ANC
    picked = pl.pallas_call(
        pick_kernel,
        out_shape=jax.ShapeDtypeStruct((count, HD), jnp.bfloat16),
        name="pick",
    )(wide_anc, gathered.reshape(NODES * KVH, HD))
    kv = lax.all_to_all(picked, ("leaf", "head"), split_axis=0, concat_axis=0, tiled=True)
    attended, query_grad, terms = attend(leaf, ancestry, node_len, query_in, out_grad, kv)
    terms = lax.all_to_all(terms, ("leaf", "head"), split_axis=0, concat_axis=0, tiled=True)
    code = ancestry[:, None, :] * KVH + jnp.arange(KVH, dtype=jnp.int32)[None, :, None]
    summed = pl.pallas_call(
        add_kernel,
        out_shape=jax.ShapeDtypeStruct((NODES * KVH, HD), jnp.bfloat16),
        name="add",
    )(code.reshape(1, count), terms)
    back = lax.all_to_all(summed.reshape(NODES, KVH, HD), "leaf", split_axis=0, concat_axis=0, tiled=True)
    back = back.reshape(rows, 2, KVH * HD).astype(jnp.float32)
    return (attended, query_grad, back[:, 0], back[:, 1])


def solution(mesh):
    return jax.shard_map(
        per_device,
        mesh=mesh,
        in_specs=(
            P("leaf", "head"),
            P(("leaf", "head"), None),
            P(("leaf", "head"), None),
            P("leaf", "head"),
            P(),
            P(),
        ),
        out_specs=(
            P("leaf", "head"),
            P("leaf", "head"),
            P(("leaf", "head"), None),
            P(("leaf", "head"), None),
        ),
        check_vma=False,
    )
```

```python
import functools

import jax
import jax.numpy as jnp
from jax import lax
from jax.experimental import pallas as pl
from jax.experimental.pallas import tpu as pltpu
from jax.sharding import PartitionSpec as P

QH = 64
KVH = 8
HD = 128
BLK = 128
ANC = 8
NODES = 32
GROUP = QH // KVH
PAIR = 2
CHUNK = 128
SIZES = (4, 5, 6, 8)
LOG2E = 1.4426950408889634
SCALE = HD ** (-0.5)
FAR = -1e30

NT = (((1,), (1,)), ((), ()))
NN = (((1,), (0,)), ((), ()))


def dot(a, b, dims=NN):
    return lax.dot_general(a, b, dims, preferred_element_type=jnp.float32)


def pick_kernel(slots, anc_ref, rows_ref, out_ref):
    for l in range(NODES):
        for s in range(slots):
            node = jnp.maximum(anc_ref[l, s], 0)
            block = rows_ref[pl.ds(pl.multiple_of(node * KVH, KVH), KVH), :]
            out_ref[pl.ds((l * slots + s) * KVH, KVH), :] = block.astype(jnp.bfloat16)


def add_kernel(code_ref, terms_ref, out_ref):
    row = lax.broadcasted_iota(jnp.int32, (NODES * KVH, terms_ref.shape[0]), 0)
    onehot = jnp.where(code_ref[...] == row, 1.0, 0.0).astype(jnp.bfloat16)
    out_ref[...] = dot(onehot, terms_ref[...])


def attention_kernel(
    slots, leaf_ref, anc_ref, len_ref, q_ref, g_ref, kv_ref, out_ref, qg_ref, kvg_ref,
    k_ref, v_ref, kt_ref, vt_ref, b_ref, e_ref, p_ref, dl_ref, qa_ref, ga_ref,
):
    step = pl.program_id(0)
    leaf = leaf_ref[0]
    wide = PAIR * BLK
    keys = slots * BLK
    band = slots * KVH

    @pl.when(step == 0)
    def _():
        for rr in range(16):
            k_ref[pl.ds(rr * band, band), :] = kv_ref[pl.ds(2 * rr * band, band), :]
            v_ref[pl.ds(rr * band, band), :] = kv_ref[pl.ds((2 * rr + 1) * band, band), :]
        kt_ref[...] = k_ref[...].T
        vt_ref[...] = v_ref[...].T
        place = lax.broadcasted_iota(jnp.int32, (KVH, BLK), 0) * 16
        query = lax.broadcasted_iota(jnp.int32, (KVH, BLK), 1)
        for s in range(slots):
            node = anc_ref[leaf, s]
            length = jnp.where(node >= 0, len_ref[jnp.maximum(node, 0)], 0)
            ends = jnp.where(node == leaf, jnp.minimum(query + 1, length), length) - place
            for rr in range(16):
                b_ref[pl.ds(rr * band + s * KVH, KVH), :] = jnp.where(rr < ends, 0.0, FAR)

    q2 = jnp.concatenate([q_ref[:, :HD], q_ref[:, HD:]], axis=0)
    g2 = jnp.concatenate([g_ref[:, :HD], g_ref[:, HD:]], axis=0)
    qa_ref[pl.ds(step * wide, wide), :] = q2
    ga_ref[pl.ds(step * wide, wide), :] = g2

    top = jnp.full((KVH, wide), FAR, jnp.float32)
    for c in range(keys // CHUNK):
        rows = pl.ds(c * CHUNK, CHUNK)
        bias = b_ref[rows, :]
        raw = dot(k_ref[rows, :], q2, NT) * (SCALE * LOG2E) + jnp.concatenate([bias, bias], axis=1)
        top = jnp.maximum(top, jnp.max(raw.reshape(CHUNK // KVH, KVH, wide), axis=0))
        e_ref[rows, :] = raw
    row_top = jnp.max(top, axis=0, keepdims=True)
    part = jnp.zeros((KVH, wide), jnp.float32)
    acc = jnp.zeros((HD, wide), jnp.float32)
    for c in range(keys // CHUNK):
        rows = pl.ds(c * CHUNK, CHUNK)
        expo = jnp.exp2(e_ref[rows, :] - row_top)
        e_ref[rows, :] = expo
        part = part + jnp.sum(expo.reshape(CHUNK // KVH, KVH, wide), axis=0)
        acc = acc + dot(vt_ref[:, rows], expo.astype(jnp.bfloat16))
    total = jnp.sum(part, axis=0, keepdims=True)
    inverse = 1.0 / total
    out_t = (acc * inverse).astype(jnp.bfloat16)
    gt = g2.T
    delta = jnp.sum(gt.astype(jnp.float32) * out_t.astype(jnp.float32), axis=0, keepdims=True)
    for i in range(PAIR):
        out_ref[:, pl.ds(i * HD, HD)] = out_t[:, i * BLK : (i + 1) * BLK].T
    qacc = jnp.zeros((HD, wide), jnp.float32)
    for c in range(keys // CHUNK):
        rows = pl.ds(c * CHUNK, CHUNK)
        dprob = dot(v_ref[rows, :], g2, NT)
        weights = e_ref[rows, :] * inverse
        dlogit = (weights * (dprob - delta)).astype(jnp.bfloat16)
        p_ref[step, rows, :] = weights.astype(jnp.bfloat16)
        dl_ref[step, rows, :] = dlogit
        qacc = qacc + dot(kt_ref[:, rows], dlogit)
    qacc = qacc * SCALE
    for i in range(PAIR):
        qg_ref[:, pl.ds(i * HD, HD)] = qacc[:, i * BLK : (i + 1) * BLK].T

    @pl.when(step == pl.num_programs(0) - 1)
    def _():
        for rr in range(16):
            rows = pl.ds(rr * band, band)
            kg = jnp.zeros((band, HD), jnp.float32)
            vg = jnp.zeros((band, HD), jnp.float32)
            for b in range(GROUP // PAIR):
                kg = kg + dot(dl_ref[b, rows, :], qa_ref[pl.ds(b * wide, wide), :])
                vg = vg + dot(p_ref[b, rows, :], ga_ref[pl.ds(b * wide, wide), :])
            kvg_ref[pl.ds(2 * rr * band, band), :] = (kg * SCALE).astype(jnp.bfloat16)
            kvg_ref[pl.ds((2 * rr + 1) * band, band), :] = vg.astype(jnp.bfloat16)


def attend(slots, leaf, ancestry, node_len, query, grad, kv):
    wide = PAIR * HD
    keys = slots * BLK
    whole = lambda shape: pl.BlockSpec(shape, lambda i, *_: (0,) * len(shape))
    pair = lambda: pl.BlockSpec((BLK, wide), lambda i, *_: (0, i))
    steps = GROUP // PAIR
    return pl.pallas_call(
        functools.partial(attention_kernel, slots),
        out_shape=(
            jax.ShapeDtypeStruct((BLK, GROUP * HD), jnp.bfloat16),
            jax.ShapeDtypeStruct((BLK, GROUP * HD), jnp.float32),
            jax.ShapeDtypeStruct((2 * keys, HD), jnp.bfloat16),
        ),
        grid_spec=pltpu.PrefetchScalarGridSpec(
            num_scalar_prefetch=3,
            grid=(steps,),
            in_specs=[pair(), pair(), pl.BlockSpec(memory_space=pltpu.VMEM)],
            out_specs=[pair(), pair(), whole((2 * keys, HD))],
            scratch_shapes=[
                pltpu.VMEM((keys, HD), jnp.bfloat16),
                pltpu.VMEM((keys, HD), jnp.bfloat16),
                pltpu.VMEM((HD, keys), jnp.bfloat16),
                pltpu.VMEM((HD, keys), jnp.bfloat16),
                pltpu.VMEM((keys, BLK), jnp.float32),
                pltpu.VMEM((keys, PAIR * BLK), jnp.float32),
                pltpu.VMEM((steps, keys, PAIR * BLK), jnp.bfloat16),
                pltpu.VMEM((steps, keys, PAIR * BLK), jnp.bfloat16),
                pltpu.VMEM((GROUP * BLK, HD), jnp.bfloat16),
                pltpu.VMEM((GROUP * BLK, HD), jnp.bfloat16),
            ],
        ),
        compiler_params=pltpu.CompilerParams(dimension_semantics=("arbitrary",)),
        name=f"attend{slots}",
    )(leaf, ancestry, node_len, query, grad, kv)


def near(x):
    return pltpu.with_memory_space_constraint(x, pltpu.VMEM)


def exchange(slots, leaf, ancestry, node_len, query, grad, rows):
    count = NODES * slots * KVH
    picked = pl.pallas_call(
        functools.partial(pick_kernel, slots),
        out_shape=jax.ShapeDtypeStruct((count, HD), jnp.bfloat16),
        in_specs=[pl.BlockSpec(memory_space=pltpu.SMEM), pl.BlockSpec(memory_space=pltpu.VMEM)],
        name=f"pick{slots}",
    )(ancestry, near(rows))
    kv = lax.all_to_all(picked, "leaf", split_axis=0, concat_axis=0, tiled=True)
    attended, query_grad, terms = attend(slots, leaf, ancestry, node_len, query, grad, near(kv))
    terms = lax.all_to_all(terms, "leaf", split_axis=0, concat_axis=0, tiled=True)
    code = ancestry[:, :slots, None] * KVH + jnp.arange(KVH, dtype=jnp.int32)
    summed = pl.pallas_call(
        add_kernel,
        out_shape=jax.ShapeDtypeStruct((NODES * KVH, HD), jnp.float32),
        name=f"add{slots}",
    )(code.reshape(1, count), near(terms))
    return attended, query_grad, summed


def per_device(query_in, key_in, value_in, out_grad, ancestry, node_len):
    everyone = ("leaf", "head")
    leaf = lax.axis_index("leaf").astype(jnp.int32).reshape(1)
    rows = key_in.shape[0]
    pieces = jnp.stack([key_in.reshape(rows, KVH, HD), value_in.reshape(rows, KVH, HD)], axis=1)
    pieces = pieces.reshape(2 * rows * KVH, HD).astype(jnp.float32)
    gathered = lax.all_to_all(pieces, everyone, split_axis=0, concat_axis=0, tiled=True)
    used = jnp.max(jnp.sum((ancestry >= 0).astype(jnp.int32), axis=1))
    index = sum((used > size).astype(jnp.int32) for size in SIZES[:-1])
    branches = [functools.partial(exchange, size) for size in SIZES]
    args = (leaf, ancestry, node_len, query_in, out_grad, gathered)
    if len(SIZES) == 1:
        attended, query_grad, summed = branches[0](*args)
    else:
        attended, query_grad, summed = lax.switch(index, branches, *args)
    back = lax.all_to_all(summed, everyone, split_axis=0, concat_axis=0, tiled=True)
    back = back.reshape(rows, 2, KVH * HD)
    return (attended, query_grad, back[:, 0], back[:, 1])


def solution(mesh):
    return jax.shard_map(
        per_device,
        mesh=mesh,
        in_specs=(
            P("leaf", "head"),
            P(("leaf", "head"), None),
            P(("leaf", "head"), None),
            P("leaf", "head"),
            P(),
            P(),
        ),
        out_specs=(
            P("leaf", "head"),
            P("leaf", "head"),
            P(("leaf", "head"), None),
            P(("leaf", "head"), None),
        ),
        check_vma=False,
    )
```

```python
import jax
import jax.numpy as jnp
from jax import lax
from jax.experimental import pallas as pl
from jax.experimental.pallas import tpu as pltpu
from jax.sharding import Mesh, PartitionSpec as P

QH = 64
KVH = 8
HD = 128
BLK = 128
ANC = 8
NODES = 32
GROUP = QH // KVH
FAR = 4
NEAR = 8
PIECE = 4
SHARE = KVH * PIECE
QUADS = 16 // PIECE
WIDE = GROUP * BLK
STRIP = 256
LOG2E = 1.4426950408889634
SCALE = HD ** (-0.5)
LOW = -1e30

NT = (((1,), (1,)), ((), ()))
NN = (((1,), (0,)), ((), ()))


def dot(a, b, dims=NN):
    return lax.dot_general(a, b, dims, preferred_element_type=jnp.float32)


def pick_kernel(leaf_ref, anc_ref, rows_ref, out_ref):
    base = (leaf_ref[0] // NEAR) * NEAR
    for j in range(NEAR):
        for s in range(ANC):
            node = jnp.maximum(anc_ref[s, base + j], 0)
            first = pl.multiple_of(node * SHARE, SHARE)
            out_ref[pl.ds((j * ANC + s) * SHARE, SHARE), :] = rows_ref[pl.ds(first, SHARE), :]


def add_kernel(leaf_ref, anc_ref, terms_ref, out_ref, sum_ref):
    base = (leaf_ref[0] // NEAR) * NEAR
    sum_ref[...] = jnp.zeros_like(sum_ref)
    for j in range(NEAR):
        for s in range(ANC):
            node = anc_ref[s, base + j]
            node = jnp.where(node >= 0, node, NODES)
            here = pl.ds(pl.multiple_of(node * SHARE, SHARE), SHARE)
            term = terms_ref[pl.ds((j * ANC + s) * SHARE, SHARE), :].astype(jnp.float32)
            sum_ref[here, :] = sum_ref[here, :] + term
    out_ref[...] = sum_ref[: NODES * SHARE, :].astype(jnp.bfloat16)


def finish_kernel(back_ref, key_ref, value_ref):
    part = NEAR * SHARE
    total = back_ref[:part, :].astype(jnp.float32)
    for f in range(1, FAR):
        total = total + back_ref[f * part : (f + 1) * part, :].astype(jnp.float32)
    for kind, ref in ((0, key_ref), (1, value_ref)):
        for h in range(KVH):
            rows = []
            for quad in range(QUADS):
                first = (quad * 2 + kind) * SHARE + h * PIECE
                rows.append(total[first : first + PIECE])
            ref[:, h * HD : (h + 1) * HD] = jnp.concatenate(rows, axis=0)


def attention_kernel(
    leaf_ref, anc_ref, len_ref, q_ref, g_ref, kv_ref, out_ref, qg_ref, kvg_ref,
    qa_ref, ga_ref, gt_ref, e_ref, top_ref, sum_ref, acc_ref,
):
    leaf = leaf_ref[0]
    used = jnp.int32(0)
    for s in range(ANC):
        used = used + jnp.where(anc_ref[s, leaf] >= 0, 1, 0)

    for h in range(GROUP):
        qa_ref[h * BLK : (h + 1) * BLK, :] = q_ref[:, h * HD : (h + 1) * HD]
        g = g_ref[:, h * HD : (h + 1) * HD]
        ga_ref[h * BLK : (h + 1) * BLK, :] = g
        gt_ref[:, h * BLK : (h + 1) * BLK] = g.T
    top_ref[...] = jnp.full_like(top_ref, LOW)
    sum_ref[...] = jnp.zeros_like(sum_ref)
    acc_ref[...] = jnp.zeros_like(acc_ref)

    row = lax.broadcasted_iota(jnp.int32, (BLK, BLK), 0)
    place = ((row // PIECE) % KVH) * 16 + (row // SHARE) * PIECE + row % PIECE
    query = lax.broadcasted_iota(jnp.int32, (BLK, BLK), 1)

    def keys_of(s, kind):
        return jnp.concatenate(
            [
                kv_ref[pl.ds(pl.multiple_of(((2 * quad + kind) * ANC + s) * SHARE, SHARE), SHARE), :]
                for quad in range(QUADS)
            ],
            axis=0,
        )

    strips = [slice(i * STRIP, (i + 1) * STRIP) for i in range(WIDE // STRIP)]

    def logits_pass(s, carry):
        node = anc_ref[s, leaf]
        length = len_ref[node]
        ends = jnp.where(node == leaf, jnp.minimum(query + 1, length), length)
        seen = jnp.concatenate([place < ends] * (STRIP // BLK), axis=1)
        key = keys_of(s, 0)
        for strip in strips:
            raw = dot(key, qa_ref[strip, :], NT) * (SCALE * LOG2E)
            raw = jnp.where(seen, raw, LOW)
            e_ref[s, :, strip] = raw
            high = jnp.max(raw.reshape(BLK // 8, 8, STRIP), axis=0)
            top_ref[:, strip] = jnp.maximum(top_ref[:, strip], high)
        return carry

    lax.fori_loop(0, used, logits_pass, 0)
    top_ref[...] = jnp.broadcast_to(jnp.max(top_ref[...], axis=0, keepdims=True), top_ref.shape)

    def output_pass(s, carry):
        value_t = keys_of(s, 1).T
        for strip in strips:
            expo = jnp.exp2(e_ref[s, :, strip] - top_ref[:1, strip])
            e_ref[s, :, strip] = expo
            sum_ref[:, strip] = sum_ref[:, strip] + jnp.sum(expo.reshape(BLK // 8, 8, STRIP), axis=0)
            acc_ref[:, strip] = acc_ref[:, strip] + dot(value_t, expo.astype(jnp.bfloat16))
        return carry

    lax.fori_loop(0, used, output_pass, 0)
    for strip in strips:
        inverse = 1.0 / jnp.sum(sum_ref[:, strip], axis=0, keepdims=True)
        out_t = (acc_ref[:, strip] * inverse).astype(jnp.bfloat16)
        delta = jnp.sum(gt_ref[:, strip].astype(jnp.float32) * out_t.astype(jnp.float32), axis=0, keepdims=True)
        top_ref[:1, strip] = inverse
        sum_ref[:1, strip] = delta
        out = out_t.T
        for i in range(STRIP // BLK):
            first = strip.start + i * BLK
            out_ref[:, first : first + BLK] = out[i * BLK : (i + 1) * BLK, :]
    acc_ref[...] = jnp.zeros_like(acc_ref)

    def gradient_pass(s, carry):
        key_t = keys_of(s, 0).T
        value = keys_of(s, 1)
        key_sum = jnp.zeros((BLK, HD), jnp.float32)
        value_sum = jnp.zeros((BLK, HD), jnp.float32)
        for strip in strips:
            dprob = dot(value, gt_ref[:, strip])
            weights = e_ref[s, :, strip] * top_ref[:1, strip]
            dlogit = (weights * (dprob - sum_ref[:1, strip])).astype(jnp.bfloat16)
            value_sum = value_sum + dot(weights.astype(jnp.bfloat16), ga_ref[strip, :])
            key_sum = key_sum + dot(dlogit, qa_ref[strip, :])
            acc_ref[:, strip] = acc_ref[:, strip] + dot(key_t, dlogit)
        for kind, total in ((0, key_sum * SCALE), (1, value_sum)):
            total = total.astype(jnp.bfloat16)
            for quad in range(QUADS):
                first = pl.multiple_of(((2 * quad + kind) * ANC + s) * SHARE, SHARE)
                kvg_ref[pl.ds(first, SHARE), :] = total[quad * SHARE : (quad + 1) * SHARE]
        return carry

    lax.fori_loop(0, used, gradient_pass, 0)
    for strip in strips:
        grad = (acc_ref[:, strip] * SCALE).T
        for i in range(STRIP // BLK):
            first = strip.start + i * BLK
            qg_ref[:, first : first + BLK] = grad[i * BLK : (i + 1) * BLK, :]


def near_memory(x):
    return pltpu.with_memory_space_constraint(x, pltpu.VMEM)


SMEM = pl.BlockSpec(memory_space=pltpu.SMEM)
VMEM = pl.BlockSpec(memory_space=pltpu.VMEM)


def attend(leaf, ancestry_t, node_len, query, grad, kv):
    return pl.pallas_call(
        attention_kernel,
        out_shape=(
            jax.ShapeDtypeStruct((BLK, GROUP * HD), jnp.bfloat16),
            jax.ShapeDtypeStruct((BLK, GROUP * HD), jnp.float32),
            jax.ShapeDtypeStruct((2 * ANC * BLK, HD), jnp.bfloat16),
        ),
        in_specs=[SMEM, SMEM, SMEM, VMEM, VMEM, VMEM],
        out_specs=(VMEM, VMEM, VMEM),
        scratch_shapes=[
            pltpu.VMEM((WIDE, HD), jnp.bfloat16),
            pltpu.VMEM((WIDE, HD), jnp.bfloat16),
            pltpu.VMEM((HD, WIDE), jnp.bfloat16),
            pltpu.VMEM((ANC, BLK, WIDE), jnp.float32),
            pltpu.VMEM((8, WIDE), jnp.float32),
            pltpu.VMEM((8, WIDE), jnp.float32),
            pltpu.VMEM((HD, WIDE), jnp.float32),
        ],
        name="attend",
    )(leaf, ancestry_t, node_len, near_memory(query), near_memory(grad), near_memory(kv))


def per_device(query_in, key_in, value_in, out_grad, ancestry, node_len):
    everyone = ("far", "near", "head")
    leaf = (lax.axis_index("far") * NEAR + lax.axis_index("near")).astype(jnp.int32).reshape(1)
    ancestry_t = ancestry.T
    rows = key_in.shape[0]

    def cut(x):
        return x.reshape(QUADS, PIECE, KVH, HD).transpose(0, 2, 1, 3)

    pieces = jnp.stack([cut(key_in), cut(value_in)], axis=1).reshape(1, NEAR * SHARE, HD)
    pieces = jnp.broadcast_to(pieces, (FAR, NEAR * SHARE, HD)).reshape(FAR * NEAR * SHARE, HD)
    shares = lax.all_to_all(pieces, everyone, split_axis=0, concat_axis=0, tiled=True)
    picked = pl.pallas_call(
        pick_kernel,
        out_shape=jax.ShapeDtypeStruct((NEAR * ANC * SHARE, HD), jnp.bfloat16),
        in_specs=[SMEM, SMEM, VMEM],
        out_specs=VMEM,
        name="pick",
    )(leaf, ancestry_t, near_memory(shares))
    kv = lax.all_to_all(picked, "near", split_axis=0, concat_axis=0, tiled=True)
    attended, query_grad, terms = attend(leaf, ancestry_t, node_len, query_in, out_grad, kv)
    terms = lax.all_to_all(terms, "near", split_axis=0, concat_axis=0, tiled=True)
    summed = pl.pallas_call(
        add_kernel,
        out_shape=jax.ShapeDtypeStruct((NODES * SHARE, HD), jnp.bfloat16),
        in_specs=[SMEM, SMEM, VMEM],
        out_specs=VMEM,
        scratch_shapes=[pltpu.VMEM(((NODES + 1) * SHARE, HD), jnp.float32)],
        name="add",
    )(leaf, ancestry_t, near_memory(terms))
    back = lax.all_to_all(summed, everyone, split_axis=0, concat_axis=0, tiled=True)
    key_grad, value_grad = pl.pallas_call(
        finish_kernel,
        out_shape=(
            jax.ShapeDtypeStruct((rows, KVH * HD), jnp.float32),
            jax.ShapeDtypeStruct((rows, KVH * HD), jnp.float32),
        ),
        in_specs=[VMEM],
        out_specs=(VMEM, VMEM),
        name="finish",
    )(near_memory(back))
    return (attended, query_grad, key_grad, value_grad)


def solution(mesh):
    mesh = Mesh(mesh.devices.reshape(FAR, NEAR, KVH), ("far", "near", "head"))
    leaf = ("far", "near")
    token = ("far", "near", "head")
    return jax.shard_map(
        per_device,
        mesh=mesh,
        in_specs=(P(leaf, "head"), P(token, None), P(token, None), P(leaf, "head"), P(), P()),
        out_specs=(P(leaf, "head"), P(leaf, "head"), P(token, None), P(token, None)),
        check_vma=False,
    )
```

```python
import jax
import jax.numpy as jnp
from jax import lax
from jax.experimental import pallas as pl
from jax.experimental.pallas import tpu as pltpu
from jax.sharding import Mesh, PartitionSpec as P

QH = 64
KVH = 8
HD = 128
BLK = 128
ANC = 8
NODES = 32
GROUP = QH // KVH
FAR = 4
NEAR = 8
PIECE = 4
SHARE = KVH * PIECE
QUADS = 16 // PIECE
WIDE = GROUP * BLK
STRIP = 256
LOG2E = 1.4426950408889634
SCALE = HD ** (-0.5)
LOW = -1e30

NT = (((1,), (1,)), ((), ()))
NN = (((1,), (0,)), ((), ()))


def dot(a, b, dims=NN):
    return lax.dot_general(a, b, dims, preferred_element_type=jnp.float32)


def cut_kernel(key_ref, value_ref, out_ref):
    for kind, ref in ((0, key_ref), (1, value_ref)):
        rows = ref[...].astype(jnp.float32)
        for quad in range(QUADS):
            part = rows[quad * PIECE : (quad + 1) * PIECE]
            share = jnp.concatenate([part[:, h * HD : (h + 1) * HD] for h in range(KVH)], axis=0)
            share = share.astype(jnp.bfloat16)
            for f in range(FAR):
                first = (f * NEAR + quad * 2 + kind) * SHARE
                out_ref[first : first + SHARE, :] = share


def prep_kernel(q_ref, g_ref, out_ref):
    for h in range(GROUP):
        here = slice(h * HD, (h + 1) * HD)
        g = g_ref[:, here]
        for part, block in enumerate((q_ref[:, here], g, g.T)):
            first = part * WIDE + h * BLK
            out_ref[first : first + BLK, :] = block


def pick_kernel(leaf_ref, anc_ref, rows_ref, out_ref, sem):
    base = (leaf_ref[0] // NEAR) * NEAR
    for j in range(NEAR):
        for s in range(ANC):
            node = jnp.maximum(anc_ref[s, base + j], 0)
            first = pl.multiple_of(node * SHARE, SHARE)
            to = out_ref.at[pl.ds((j * ANC + s) * SHARE, SHARE), :]
            pltpu.make_async_copy(rows_ref.at[pl.ds(first, SHARE), :], to, sem).start()
    pltpu.make_async_copy(out_ref, out_ref, sem).wait()


def add_kernel(leaf_ref, anc_ref, terms_ref, out_ref, even_ref, odd_ref):
    base = (leaf_ref[0] // NEAR) * NEAR

    def term(j, s):
        first = (j * ANC + s) * SHARE
        return terms_ref[first : first + SHARE, :].astype(jnp.float32)

    root = term(0, 0)
    for j in range(1, NEAR):
        root = root + term(j, 0)
    even_ref[:SHARE, :] = root
    even_ref[SHARE:, :] = jnp.zeros_like(even_ref[SHARE:, :])
    odd_ref[...] = jnp.zeros_like(odd_ref)
    for s in range(1, ANC):
        nodes = [anc_ref[s, base + j] for j in range(NEAR)]
        highest = nodes[0]
        for node in nodes[1:]:
            highest = jnp.maximum(highest, node)

        @pl.when(highest >= 0)
        def _():
            for j, node in enumerate(nodes):
                ref = odd_ref if j % 2 else even_ref
                place = jnp.where(node >= 0, node, NODES)
                here = pl.ds(pl.multiple_of(place * SHARE, SHARE), SHARE)
                ref[here, :] = ref[here, :] + term(j, s)

    rows = NODES * SHARE
    out_ref[...] = (even_ref[:rows, :] + odd_ref[:rows, :]).astype(jnp.bfloat16)


def finish_kernel(back_ref, key_ref, value_ref):
    part = NEAR * SHARE
    total = back_ref[:part, :].astype(jnp.float32)
    for f in range(1, FAR):
        total = total + back_ref[f * part : (f + 1) * part, :].astype(jnp.float32)
    for kind, ref in ((0, key_ref), (1, value_ref)):
        for h in range(KVH):
            rows = []
            for quad in range(QUADS):
                first = (quad * 2 + kind) * SHARE + h * PIECE
                rows.append(total[first : first + PIECE])
            ref[:, h * HD : (h + 1) * HD] = jnp.concatenate(rows, axis=0)


def keys_of(kv_ref, s, kind):
    firsts = [((2 * quad + kind) * ANC + s) * SHARE for quad in range(QUADS)]
    return jnp.concatenate([kv_ref[pl.ds(pl.multiple_of(f, SHARE), SHARE), :] for f in firsts], axis=0)


def used_slots(anc_ref, leaf):
    used = jnp.int32(0)
    for s in range(ANC):
        used = used + jnp.where(anc_ref[s, leaf] >= 0, 1, 0)
    return used


STRIPS = [slice(i * STRIP, (i + 1) * STRIP) for i in range(WIDE // STRIP)]


def attention_kernel(
    leaf_ref, anc_ref, len_ref, in_ref, kv_ref, kvg_ref, dl_ref, out_ref,
    e_ref, top_ref, sum_ref, acc_ref,
):
    leaf = leaf_ref[0]
    used = used_slots(anc_ref, leaf)

    def stacked(part, strip):
        return in_ref[part * WIDE + strip.start : part * WIDE + strip.stop, :]

    def turned(strip):
        rows = stacked(2, strip)
        return jnp.concatenate([rows[i * HD : (i + 1) * HD] for i in range(STRIP // BLK)], axis=1)

    top_ref[...] = jnp.full_like(top_ref, LOW)
    sum_ref[...] = jnp.zeros_like(sum_ref)
    acc_ref[...] = jnp.zeros_like(acc_ref)

    row = lax.broadcasted_iota(jnp.int32, (BLK, BLK), 0)
    place = ((row // PIECE) % KVH) * 16 + (row // SHARE) * PIECE + row % PIECE
    query = lax.broadcasted_iota(jnp.int32, (BLK, BLK), 1)

    def logits_pass(s, carry):
        node = anc_ref[s, leaf]
        length = len_ref[node]
        ends = jnp.where(node == leaf, jnp.minimum(query + 1, length), length)
        seen = jnp.concatenate([place < ends] * (STRIP // BLK), axis=1)
        key = keys_of(kv_ref, s, 0)
        for strip in STRIPS:
            raw = dot(key, stacked(0, strip), NT) * (SCALE * LOG2E)
            raw = jnp.where(seen, raw, LOW)
            e_ref[s, :, strip] = raw
            high = jnp.max(raw.reshape(BLK // 8, 8, STRIP), axis=0)
            top_ref[:, strip] = jnp.maximum(top_ref[:, strip], high)
        return carry

    lax.fori_loop(0, used, logits_pass, 0)
    top_ref[...] = jnp.broadcast_to(jnp.max(top_ref[...], axis=0, keepdims=True), top_ref.shape)

    def output_pass(s, carry):
        value_t = keys_of(kv_ref, s, 1).T
        for strip in STRIPS:
            expo = jnp.exp2(e_ref[s, :, strip] - top_ref[:1, strip])
            e_ref[s, :, strip] = expo
            sum_ref[:, strip] = sum_ref[:, strip] + jnp.sum(expo.reshape(BLK // 8, 8, STRIP), axis=0)
            acc_ref[:, strip] = acc_ref[:, strip] + dot(value_t, expo.astype(jnp.bfloat16))
        return carry

    lax.fori_loop(0, used, output_pass, 0)
    for strip in STRIPS:
        inverse = 1.0 / jnp.sum(sum_ref[:, strip], axis=0, keepdims=True)
        out_t = (acc_ref[:, strip] * inverse).astype(jnp.bfloat16)
        delta = jnp.sum(turned(strip).astype(jnp.float32) * out_t.astype(jnp.float32), axis=0, keepdims=True)
        top_ref[:1, strip] = inverse
        sum_ref[:1, strip] = delta
        out_ref[:, strip] = out_t

    def gradient_pass(s, carry):
        value = keys_of(kv_ref, s, 1)
        key_sum = jnp.zeros((BLK, HD), jnp.float32)
        value_sum = jnp.zeros((BLK, HD), jnp.float32)
        for strip in STRIPS:
            dprob = dot(value, turned(strip))
            weights = e_ref[s, :, strip] * top_ref[:1, strip]
            dlogit = (weights * (dprob - sum_ref[:1, strip])).astype(jnp.bfloat16)
            value_sum = value_sum + dot(weights.astype(jnp.bfloat16), stacked(1, strip))
            key_sum = key_sum + dot(dlogit, stacked(0, strip))
            dl_ref[s, :, strip] = dlogit
        for kind, total in ((0, key_sum * SCALE), (1, value_sum)):
            total = total.astype(jnp.bfloat16)
            for quad in range(QUADS):
                first = pl.multiple_of(((2 * quad + kind) * ANC + s) * SHARE, SHARE)
                kvg_ref[pl.ds(first, SHARE), :] = total[quad * SHARE : (quad + 1) * SHARE]
        return carry

    lax.fori_loop(0, used, gradient_pass, 0)

def late_kernel(leaf_ref, anc_ref, kv_ref, dl_ref, out_t_ref, out_ref, qg_ref, acc_ref):
    used = used_slots(anc_ref, leaf_ref[0])
    for h in range(GROUP):
        here = slice(h * BLK, (h + 1) * BLK)
        out_ref[:, here] = out_t_ref[:, here].T
    acc_ref[...] = jnp.zeros_like(acc_ref)

    def query_pass(s, carry):
        key_t = keys_of(kv_ref, s, 0).T
        for strip in STRIPS:
            acc_ref[:, strip] = acc_ref[:, strip] + dot(key_t, dl_ref[s, :, strip])
        return carry

    lax.fori_loop(0, used, query_pass, 0)
    for h in range(GROUP):
        here = slice(h * BLK, (h + 1) * BLK)
        qg_ref[:, here] = (acc_ref[:, here] * SCALE).T


def near_memory(x):
    return pltpu.with_memory_space_constraint(x, pltpu.VMEM)


SMEM = pl.BlockSpec(memory_space=pltpu.SMEM)
VMEM = pl.BlockSpec(memory_space=pltpu.VMEM)


ANY = pl.BlockSpec(memory_space=pl.ANY)


def room(mebibytes):
    return pltpu.CompilerParams(vmem_limit_bytes=mebibytes << 20)


def shaped(shape, dtype):
    return jax.ShapeDtypeStruct(shape, dtype)


def per_device(query_in, key_in, value_in, out_grad, ancestry, node_len):
    everyone = ("far", "near", "head")
    leaf = (lax.axis_index("far") * NEAR + lax.axis_index("near")).astype(jnp.int32).reshape(1)
    ancestry_t = ancestry.T
    rows = key_in.shape[0]

    low, wide = jnp.bfloat16, jnp.float32
    pieces = pl.pallas_call(
        cut_kernel,
        out_shape=shaped((FAR * NEAR * SHARE, HD), low),
        in_specs=[VMEM, VMEM],
        out_specs=VMEM,
        compiler_params=room(4),
        name="cut",
    )(key_in, value_in)
    shares = lax.all_to_all(pieces, everyone, split_axis=0, concat_axis=0, tiled=True)
    stacked = pl.pallas_call(
        prep_kernel,
        out_shape=pltpu.VMEM((3 * WIDE, HD), low),
        in_specs=[VMEM, VMEM],
        out_specs=VMEM,
        compiler_params=room(4),
        name="prep",
    )(query_in, out_grad)
    picked = pl.pallas_call(
        pick_kernel,
        out_shape=shaped((NEAR * ANC * SHARE, HD), low),
        in_specs=[SMEM, SMEM, VMEM],
        out_specs=ANY,
        scratch_shapes=[pltpu.SemaphoreType.DMA],
        compiler_params=room(4),
        name="pick",
    )(leaf, ancestry_t, near_memory(shares))
    kv = near_memory(lax.all_to_all(picked, "near", split_axis=0, concat_axis=0, tiled=True))
    terms, dlogit, out_t = pl.pallas_call(
        attention_kernel,
        out_shape=(
            shaped((2 * ANC * BLK, HD), low),
            pltpu.VMEM((ANC, BLK, WIDE), low),
            pltpu.VMEM((HD, WIDE), low),
        ),
        in_specs=[SMEM, SMEM, SMEM, VMEM, VMEM],
        out_specs=(VMEM, VMEM, VMEM),
        scratch_shapes=[
            pltpu.VMEM((ANC, BLK, WIDE), wide),
            pltpu.VMEM((8, WIDE), wide),
            pltpu.VMEM((8, WIDE), wide),
            pltpu.VMEM((HD, WIDE), wide),
        ],
        compiler_params=room(16),
        name="attend",
    )(leaf, ancestry_t, node_len, near_memory(stacked), kv)
    terms = lax.all_to_all(terms, "near", split_axis=0, concat_axis=0, tiled=True)
    attended, query_grad = pl.pallas_call(
        late_kernel,
        out_shape=(shaped((BLK, GROUP * HD), low), shaped((BLK, GROUP * HD), wide)),
        in_specs=[SMEM, SMEM, VMEM, VMEM, VMEM],
        out_specs=(VMEM, VMEM),
        scratch_shapes=[pltpu.VMEM((HD, WIDE), wide)],
        compiler_params=room(8),
        name="late",
    )(leaf, ancestry_t, kv, near_memory(dlogit), near_memory(out_t))
    summed = pl.pallas_call(
        add_kernel,
        out_shape=shaped((NODES * SHARE, HD), low),
        in_specs=[SMEM, SMEM, VMEM],
        out_specs=VMEM,
        scratch_shapes=[
            pltpu.VMEM(((NODES + 1) * SHARE, HD), wide),
            pltpu.VMEM(((NODES + 1) * SHARE, HD), wide),
        ],
        compiler_params=room(8),
        name="add",
    )(leaf, ancestry_t, near_memory(terms))
    back = lax.all_to_all(summed, everyone, split_axis=0, concat_axis=0, tiled=True)
    key_grad, value_grad = pl.pallas_call(
        finish_kernel,
        out_shape=(shaped((rows, KVH * HD), wide), shaped((rows, KVH * HD), wide)),
        in_specs=[VMEM],
        out_specs=(VMEM, VMEM),
        compiler_params=room(8),
        name="finish",
    )(near_memory(back))
    return (attended, query_grad, key_grad, value_grad)


def solution(mesh):
    mesh = Mesh(mesh.devices.reshape(FAR, NEAR, KVH), ("far", "near", "head"))
    leaf = ("far", "near")
    token = ("far", "near", "head")
    return jax.shard_map(
        per_device,
        mesh=mesh,
        in_specs=(P(leaf, "head"), P(token, None), P(token, None), P(leaf, "head"), P(), P()),
        out_specs=(P(leaf, "head"), P(leaf, "head"), P(token, None), P(token, None)),
        check_vma=False,
    )
```

```python
import jax
import jax.numpy as jnp
from jax import lax
from jax.experimental import pallas as pl
from jax.experimental.pallas import tpu as pltpu
from jax.sharding import Mesh, PartitionSpec as P

QH = 64
KVH = 8
HD = 128
BLK = 128
ANC = 8
NODES = 32
GROUP = QH // KVH
FAR = 4
NEAR = 8
PIECE = 4
SHARE = KVH * PIECE
QUADS = 16 // PIECE
WIDE = GROUP * BLK
STRIP = 256
LOG2E = 1.4426950408889634
SCALE = HD ** (-0.5)
LOW = -1e30

NT = (((1,), (1,)), ((), ()))
NN = (((1,), (0,)), ((), ()))


def dot(a, b, dims=NN):
    return lax.dot_general(a, b, dims, preferred_element_type=jnp.float32)


def cut_kernel(key_hbm, value_hbm, out_ref, key_ref, value_ref, sems):
    kinds = ((key_hbm, key_ref), (value_hbm, value_ref))
    for kind, (far_ref, ref) in enumerate(kinds):
        pltpu.make_async_copy(far_ref, ref, sems.at[kind]).start()
    for kind, (far_ref, ref) in enumerate(kinds):
        pltpu.make_async_copy(far_ref, ref, sems.at[kind]).wait()
        rows = ref[...].astype(jnp.float32)
        for quad in range(QUADS):
            part = rows[quad * PIECE : (quad + 1) * PIECE]
            share = jnp.concatenate([part[:, h * HD : (h + 1) * HD] for h in range(KVH)], axis=0)
            share = share.astype(jnp.bfloat16)
            for f in range(FAR):
                first = (f * NEAR + quad * 2 + kind) * SHARE
                out_ref[first : first + SHARE, :] = share


def prep_kernel(q_ref, g_ref, out_ref):
    for h in range(GROUP):
        here = slice(h * HD, (h + 1) * HD)
        g = g_ref[:, here]
        for part, block in enumerate((q_ref[:, here], g, g.T)):
            first = part * WIDE + h * BLK
            out_ref[first : first + BLK, :] = block


def levels_of(leaf_ref, anc_ref):
    base = (leaf_ref[0] // NEAR) * NEAR
    for s in range(ANC):
        nodes = [anc_ref[s, base + j] for j in range(NEAR)]
        highest = nodes[0]
        for node in nodes[1:]:
            highest = jnp.maximum(highest, node)
        yield s, nodes, highest >= 0


def pick_kernel(leaf_ref, anc_ref, rows_ref, out_ref, sems):
    levels = list(levels_of(leaf_ref, anc_ref))
    for s, nodes, some in levels:

        @pl.when(some)
        def _():
            for j, node in enumerate(nodes):
                first = pl.multiple_of(jnp.maximum(node, 0) * SHARE, SHARE)
                to = out_ref.at[pl.ds((j * ANC + s) * SHARE, SHARE), :]
                pltpu.make_async_copy(rows_ref.at[pl.ds(first, SHARE), :], to, sems.at[s]).start()

    for s, nodes, some in levels:

        @pl.when(some)
        def _():
            block = out_ref.at[: NEAR * SHARE, :]
            pltpu.make_async_copy(block, block, sems.at[s]).wait()


def add_kernel(leaf_ref, anc_ref, terms_ref, out_ref, even_ref, odd_ref):
    def term(j, s):
        first = (j * ANC + s) * SHARE
        return terms_ref[first : first + SHARE, :].astype(jnp.float32)

    root = term(0, 0)
    for j in range(1, NEAR):
        root = root + term(j, 0)
    even_ref[:SHARE, :] = root
    even_ref[SHARE:, :] = jnp.zeros_like(even_ref[SHARE:, :])
    odd_ref[...] = jnp.zeros_like(odd_ref)
    for s, nodes, some in levels_of(leaf_ref, anc_ref):
        if s == 0:
            continue

        @pl.when(some)
        def _():
            for j, node in enumerate(nodes):
                ref = odd_ref if j % 2 else even_ref
                place = jnp.where(node >= 0, node, NODES)
                here = pl.ds(pl.multiple_of(place * SHARE, SHARE), SHARE)
                ref[here, :] = ref[here, :] + term(j, s)

    rows = NODES * SHARE
    out_ref[...] = (even_ref[:rows, :] + odd_ref[:rows, :]).astype(jnp.bfloat16)


def finish_kernel(back_ref, key_ref, value_ref):
    part = NEAR * SHARE
    total = back_ref[:part, :].astype(jnp.float32)
    for f in range(1, FAR):
        total = total + back_ref[f * part : (f + 1) * part, :].astype(jnp.float32)
    for kind, ref in ((0, key_ref), (1, value_ref)):
        for h in range(KVH):
            rows = []
            for quad in range(QUADS):
                first = (quad * 2 + kind) * SHARE + h * PIECE
                rows.append(total[first : first + PIECE])
            ref[:, h * HD : (h + 1) * HD] = jnp.concatenate(rows, axis=0)


def keys_of(kv_ref, s, kind):
    firsts = [((2 * quad + kind) * ANC + s) * SHARE for quad in range(QUADS)]
    return jnp.concatenate([kv_ref[pl.ds(pl.multiple_of(f, SHARE), SHARE), :] for f in firsts], axis=0)


def used_slots(anc_ref, leaf):
    used = jnp.int32(0)
    for s in range(ANC):
        used = used + jnp.where(anc_ref[s, leaf] >= 0, 1, 0)
    return used


STRIPS = [slice(i * STRIP, (i + 1) * STRIP) for i in range(WIDE // STRIP)]


def attention_kernel(
    leaf_ref, anc_ref, len_ref, in_ref, kv_ref, kvg_ref, dl_ref, out_ref,
    e_ref, top_ref, sum_ref, acc_ref,
):
    leaf = leaf_ref[0]
    used = used_slots(anc_ref, leaf)

    def stacked(part, strip):
        return in_ref[part * WIDE + strip.start : part * WIDE + strip.stop, :]

    def turned(strip):
        rows = stacked(2, strip)
        return jnp.concatenate([rows[i * HD : (i + 1) * HD] for i in range(STRIP // BLK)], axis=1)

    top_ref[...] = jnp.full_like(top_ref, LOW)
    sum_ref[...] = jnp.zeros_like(sum_ref)
    acc_ref[...] = jnp.zeros_like(acc_ref)

    row = lax.broadcasted_iota(jnp.int32, (BLK, BLK), 0)
    place = ((row // PIECE) % KVH) * 16 + (row // SHARE) * PIECE + row % PIECE
    query = lax.broadcasted_iota(jnp.int32, (BLK, BLK), 1)

    def logits_pass(s, carry):
        node = anc_ref[s, leaf]
        length = len_ref[node]
        ends = jnp.where(node == leaf, jnp.minimum(query + 1, length), length)
        seen = jnp.concatenate([place < ends] * (STRIP // BLK), axis=1)
        key = keys_of(kv_ref, s, 0)
        for strip in STRIPS:
            raw = dot(key, stacked(0, strip), NT) * (SCALE * LOG2E)
            raw = jnp.where(seen, raw, LOW)
            e_ref[s, :, strip] = raw
            high = jnp.max(raw.reshape(BLK // 8, 8, STRIP), axis=0)
            top_ref[:, strip] = jnp.maximum(top_ref[:, strip], high)
        return carry

    lax.fori_loop(0, used, logits_pass, 0)
    top_ref[...] = jnp.broadcast_to(jnp.max(top_ref[...], axis=0, keepdims=True), top_ref.shape)

    def output_pass(s, carry):
        value_t = keys_of(kv_ref, s, 1).T
        for strip in STRIPS:
            expo = jnp.exp2(e_ref[s, :, strip] - top_ref[:1, strip])
            e_ref[s, :, strip] = expo
            sum_ref[:, strip] = sum_ref[:, strip] + jnp.sum(expo.reshape(BLK // 8, 8, STRIP), axis=0)
            acc_ref[:, strip] = acc_ref[:, strip] + dot(value_t, expo.astype(jnp.bfloat16))
        return carry

    lax.fori_loop(0, used, output_pass, 0)
    for strip in STRIPS:
        inverse = 1.0 / jnp.sum(sum_ref[:, strip], axis=0, keepdims=True)
        out_t = (acc_ref[:, strip] * inverse).astype(jnp.bfloat16)
        delta = jnp.sum(turned(strip).astype(jnp.float32) * out_t.astype(jnp.float32), axis=0, keepdims=True)
        top_ref[:1, strip] = inverse
        sum_ref[:1, strip] = delta
        out_ref[:, strip] = out_t

    def gradient_pass(s, carry):
        value = keys_of(kv_ref, s, 1)
        key_sum = jnp.zeros((BLK, HD), jnp.float32)
        value_sum = jnp.zeros((BLK, HD), jnp.float32)
        for strip in STRIPS:
            dprob = dot(value, turned(strip))
            weights = e_ref[s, :, strip] * top_ref[:1, strip]
            dlogit = (weights * (dprob - sum_ref[:1, strip])).astype(jnp.bfloat16)
            value_sum = value_sum + dot(weights.astype(jnp.bfloat16), stacked(1, strip))
            key_sum = key_sum + dot(dlogit, stacked(0, strip))
            dl_ref[s, :, strip] = dlogit
        for kind, total in ((0, key_sum * SCALE), (1, value_sum)):
            total = total.astype(jnp.bfloat16)
            for quad in range(QUADS):
                first = pl.multiple_of(((2 * quad + kind) * ANC + s) * SHARE, SHARE)
                kvg_ref[pl.ds(first, SHARE), :] = total[quad * SHARE : (quad + 1) * SHARE]
        return carry

    lax.fori_loop(0, used, gradient_pass, 0)

def late_kernel(leaf_ref, anc_ref, kv_ref, dl_ref, out_t_ref, out_ref, qg_ref, acc_ref):
    used = used_slots(anc_ref, leaf_ref[0])
    for h in range(GROUP):
        here = slice(h * BLK, (h + 1) * BLK)
        out_ref[:, here] = out_t_ref[:, here].T
    acc_ref[...] = jnp.zeros_like(acc_ref)

    def query_pass(s, carry):
        key_t = keys_of(kv_ref, s, 0).T
        for strip in STRIPS:
            acc_ref[:, strip] = acc_ref[:, strip] + dot(key_t, dl_ref[s, :, strip])
        return carry

    lax.fori_loop(0, used, query_pass, 0)
    for h in range(GROUP):
        here = slice(h * BLK, (h + 1) * BLK)
        qg_ref[:, here] = (acc_ref[:, here] * SCALE).T


def near_memory(x):
    return pltpu.with_memory_space_constraint(x, pltpu.VMEM)


def far_memory(x):
    return pltpu.with_memory_space_constraint(x, pltpu.HBM)


SMEM = pl.BlockSpec(memory_space=pltpu.SMEM)
VMEM = pl.BlockSpec(memory_space=pltpu.VMEM)


ANY = pl.BlockSpec(memory_space=pl.ANY)
HBM = pl.BlockSpec(memory_space=pltpu.HBM)


def room(mebibytes):
    return pltpu.CompilerParams(vmem_limit_bytes=mebibytes << 20)


def shaped(shape, dtype):
    return jax.ShapeDtypeStruct(shape, dtype)


def per_device(query_in, key_in, value_in, out_grad, ancestry, node_len):
    everyone = ("far", "near", "head")
    leaf = (lax.axis_index("far") * NEAR + lax.axis_index("near")).astype(jnp.int32).reshape(1)
    ancestry_t, node_len = far_memory(ancestry.T), far_memory(node_len)
    rows = key_in.shape[0]

    low, wide = jnp.bfloat16, jnp.float32
    pieces = pl.pallas_call(
        cut_kernel,
        out_shape=shaped((FAR * NEAR * SHARE, HD), low),
        in_specs=[HBM, HBM],
        out_specs=VMEM,
        scratch_shapes=[
            pltpu.VMEM(key_in.shape, low),
            pltpu.VMEM(key_in.shape, low),
            pltpu.SemaphoreType.DMA((2,)),
        ],
        compiler_params=room(4),
        name="cut",
    )(far_memory(key_in), far_memory(value_in))
    shares = lax.all_to_all(pieces, everyone, split_axis=0, concat_axis=0, tiled=True)
    stacked = pl.pallas_call(
        prep_kernel,
        out_shape=pltpu.VMEM((3 * WIDE, HD), low),
        in_specs=[VMEM, VMEM],
        out_specs=VMEM,
        compiler_params=room(4),
        name="prep",
    )(query_in, out_grad)
    picked = pl.pallas_call(
        pick_kernel,
        out_shape=shaped((NEAR * ANC * SHARE, HD), low),
        in_specs=[SMEM, SMEM, VMEM],
        out_specs=ANY,
        scratch_shapes=[pltpu.SemaphoreType.DMA((ANC,))],
        compiler_params=room(4),
        name="pick",
    )(leaf, ancestry_t, near_memory(shares))
    kv = near_memory(lax.all_to_all(picked, "near", split_axis=0, concat_axis=0, tiled=True))
    terms, dlogit, out_t = pl.pallas_call(
        attention_kernel,
        out_shape=(
            shaped((2 * ANC * BLK, HD), low),
            pltpu.VMEM((ANC, BLK, WIDE), low),
            pltpu.VMEM((HD, WIDE), low),
        ),
        in_specs=[SMEM, SMEM, SMEM, VMEM, VMEM],
        out_specs=(VMEM, VMEM, VMEM),
        scratch_shapes=[
            pltpu.VMEM((ANC, BLK, WIDE), wide),
            pltpu.VMEM((8, WIDE), wide),
            pltpu.VMEM((8, WIDE), wide),
            pltpu.VMEM((HD, WIDE), wide),
        ],
        compiler_params=room(16),
        name="attend",
    )(leaf, ancestry_t, node_len, near_memory(stacked), kv)
    terms = lax.all_to_all(terms, "near", split_axis=0, concat_axis=0, tiled=True)
    attended, query_grad = pl.pallas_call(
        late_kernel,
        out_shape=(shaped((BLK, GROUP * HD), low), shaped((BLK, GROUP * HD), wide)),
        in_specs=[SMEM, SMEM, VMEM, VMEM, VMEM],
        out_specs=(VMEM, VMEM),
        scratch_shapes=[pltpu.VMEM((HD, WIDE), wide)],
        compiler_params=room(8),
        name="late",
    )(leaf, ancestry_t, kv, near_memory(dlogit), near_memory(out_t))
    summed = pl.pallas_call(
        add_kernel,
        out_shape=shaped((NODES * SHARE, HD), low),
        in_specs=[SMEM, SMEM, VMEM],
        out_specs=VMEM,
        scratch_shapes=[
            pltpu.VMEM(((NODES + 1) * SHARE, HD), wide),
            pltpu.VMEM(((NODES + 1) * SHARE, HD), wide),
        ],
        compiler_params=room(8),
        name="add",
    )(leaf, ancestry_t, near_memory(terms))
    back = lax.all_to_all(summed, everyone, split_axis=0, concat_axis=0, tiled=True)
    key_grad, value_grad = pl.pallas_call(
        finish_kernel,
        out_shape=(shaped((rows, KVH * HD), wide), shaped((rows, KVH * HD), wide)),
        in_specs=[VMEM],
        out_specs=(VMEM, VMEM),
        compiler_params=room(8),
        name="finish",
    )(near_memory(back))
    return (attended, query_grad, key_grad, value_grad)


def solution(mesh):
    mesh = Mesh(mesh.devices.reshape(FAR, NEAR, KVH), ("far", "near", "head"))
    leaf = ("far", "near")
    token = ("far", "near", "head")
    return jax.shard_map(
        per_device,
        mesh=mesh,
        in_specs=(P(leaf, "head"), P(token, None), P(token, None), P(leaf, "head"), P(), P()),
        out_specs=(P(leaf, "head"), P(leaf, "head"), P(token, None), P(token, None)),
        check_vma=False,
    )
```

```python
import jax
import jax.numpy as jnp
from jax import lax
from jax.experimental import pallas as pl
from jax.experimental.pallas import tpu as pltpu
from jax.sharding import Mesh, PartitionSpec as P

QH = 64
KVH = 8
HD = 128
BLK = 128
ANC = 8
NODES = 32
GROUP = QH // KVH
FAR = 4
NEAR = 8
PIECE = 4
SHARE = KVH * PIECE
QUADS = 16 // PIECE
WIDE = GROUP * BLK
STRIP = 256
LOG2E = 1.4426950408889634
SCALE = HD ** (-0.5)
LOW = -1e30

NT = (((1,), (1,)), ((), ()))
NN = (((1,), (0,)), ((), ()))


def dot(a, b, dims=NN):
    return lax.dot_general(a, b, dims, preferred_element_type=jnp.float32)


def cut_kernel(key_hbm, value_hbm, out_ref, key_ref, value_ref, sems):
    kinds = ((key_hbm, key_ref), (value_hbm, value_ref))
    for kind, (far_ref, ref) in enumerate(kinds):
        pltpu.make_async_copy(far_ref, ref, sems.at[kind]).start()
    for kind, (far_ref, ref) in enumerate(kinds):
        pltpu.make_async_copy(far_ref, ref, sems.at[kind]).wait()
        rows = ref[...].astype(jnp.float32)
        for quad in range(QUADS):
            part = rows[quad * PIECE : (quad + 1) * PIECE]
            share = jnp.concatenate([part[:, h * HD : (h + 1) * HD] for h in range(KVH)], axis=0)
            share = share.astype(jnp.bfloat16)
            for f in range(FAR):
                first = (f * NEAR + quad * 2 + kind) * SHARE
                out_ref[first : first + SHARE, :] = share


def table_kernel(leaf_ref, anc_ref, len_ref, out_ref):
    for n in range(NODES):
        for a in range(ANC):
            out_ref[a, n] = anc_ref[a, n]
        out_ref[ANC, n] = len_ref[n]
    out_ref[ANC + 1, 0] = leaf_ref[0]


def prep_kernel(q_ref, g_ref, out_ref):
    for h in range(GROUP):
        here = slice(h * HD, (h + 1) * HD)
        g = g_ref[:, here]
        for part, block in enumerate((q_ref[:, here], g, g.T)):
            first = part * WIDE + h * BLK
            out_ref[first : first + BLK, :] = block


def levels_of(anc_ref):
    base = (anc_ref[ANC + 1, 0] // NEAR) * NEAR
    for s in range(ANC):
        nodes = [anc_ref[s, base + j] for j in range(NEAR)]
        highest = nodes[0]
        for node in nodes[1:]:
            highest = jnp.maximum(highest, node)
        yield s, nodes, highest >= 0


def pick_kernel(anc_ref, rows_ref, out_ref, sems):
    levels = list(levels_of(anc_ref))
    for s, nodes, some in levels:

        @pl.when(some)
        def _():
            for j, node in enumerate(nodes):
                first = pl.multiple_of(jnp.maximum(node, 0) * SHARE, SHARE)
                to = out_ref.at[pl.ds((j * ANC + s) * SHARE, SHARE), :]
                pltpu.make_async_copy(rows_ref.at[pl.ds(first, SHARE), :], to, sems.at[s]).start()

    for s, nodes, some in levels:

        @pl.when(some)
        def _():
            block = out_ref.at[: NEAR * SHARE, :]
            pltpu.make_async_copy(block, block, sems.at[s]).wait()


def add_kernel(anc_ref, terms_ref, out_ref, even_ref, odd_ref):
    def term(j, s):
        first = (j * ANC + s) * SHARE
        return terms_ref[first : first + SHARE, :].astype(jnp.float32)

    root = term(0, 0)
    for j in range(1, NEAR):
        root = root + term(j, 0)
    even_ref[:SHARE, :] = root
    even_ref[SHARE:, :] = jnp.zeros_like(even_ref[SHARE:, :])
    odd_ref[...] = jnp.zeros_like(odd_ref)
    for s, nodes, some in levels_of(anc_ref):
        if s == 0:
            continue

        @pl.when(some)
        def _():
            for j, node in enumerate(nodes):
                ref = odd_ref if j % 2 else even_ref
                place = jnp.where(node >= 0, node, NODES)
                here = pl.ds(pl.multiple_of(place * SHARE, SHARE), SHARE)
                ref[here, :] = ref[here, :] + term(j, s)

    rows = NODES * SHARE
    out_ref[...] = (even_ref[:rows, :] + odd_ref[:rows, :]).astype(jnp.bfloat16)


def finish_kernel(back_ref, key_ref, value_ref):
    part = NEAR * SHARE
    total = back_ref[:part, :].astype(jnp.float32)
    for f in range(1, FAR):
        total = total + back_ref[f * part : (f + 1) * part, :].astype(jnp.float32)
    for kind, ref in ((0, key_ref), (1, value_ref)):
        for h in range(KVH):
            rows = []
            for quad in range(QUADS):
                first = (quad * 2 + kind) * SHARE + h * PIECE
                rows.append(total[first : first + PIECE])
            ref[:, h * HD : (h + 1) * HD] = jnp.concatenate(rows, axis=0)


def keys_of(kv_ref, s, kind):
    firsts = [((2 * quad + kind) * ANC + s) * SHARE for quad in range(QUADS)]
    return jnp.concatenate([kv_ref[pl.ds(pl.multiple_of(f, SHARE), SHARE), :] for f in firsts], axis=0)


def used_slots(anc_ref, leaf):
    used = jnp.int32(0)
    for s in range(ANC):
        used = used + jnp.where(anc_ref[s, leaf] >= 0, 1, 0)
    return used


STRIPS = [slice(i * STRIP, (i + 1) * STRIP) for i in range(WIDE // STRIP)]


def attention_kernel(
    anc_ref, in_ref, kv_ref, kvg_ref, dl_ref, out_ref,
    e_ref, top_ref, sum_ref, acc_ref,
):
    leaf = anc_ref[ANC + 1, 0]
    used = used_slots(anc_ref, leaf)

    def stacked(part, strip):
        return in_ref[part * WIDE + strip.start : part * WIDE + strip.stop, :]

    def turned(strip):
        rows = stacked(2, strip)
        return jnp.concatenate([rows[i * HD : (i + 1) * HD] for i in range(STRIP // BLK)], axis=1)

    top_ref[...] = jnp.full_like(top_ref, LOW)
    sum_ref[...] = jnp.zeros_like(sum_ref)
    acc_ref[...] = jnp.zeros_like(acc_ref)

    row = lax.broadcasted_iota(jnp.int32, (BLK, BLK), 0)
    place = ((row // PIECE) % KVH) * 16 + (row // SHARE) * PIECE + row % PIECE
    query = lax.broadcasted_iota(jnp.int32, (BLK, BLK), 1)

    def logits_pass(s, carry):
        node = anc_ref[s, leaf]
        length = anc_ref[ANC, node]
        ends = jnp.where(node == leaf, jnp.minimum(query + 1, length), length)
        seen = jnp.concatenate([place < ends] * (STRIP // BLK), axis=1)
        key = keys_of(kv_ref, s, 0)
        for strip in STRIPS:
            raw = dot(key, stacked(0, strip), NT) * (SCALE * LOG2E)
            raw = jnp.where(seen, raw, LOW)
            e_ref[s, :, strip] = raw
            high = jnp.max(raw.reshape(BLK // 8, 8, STRIP), axis=0)
            top_ref[:, strip] = jnp.maximum(top_ref[:, strip], high)
        return carry

    lax.fori_loop(0, used, logits_pass, 0)
    top_ref[...] = jnp.broadcast_to(jnp.max(top_ref[...], axis=0, keepdims=True), top_ref.shape)

    def output_pass(s, carry):
        value_t = keys_of(kv_ref, s, 1).T
        for strip in STRIPS:
            expo = jnp.exp2(e_ref[s, :, strip] - top_ref[:1, strip])
            e_ref[s, :, strip] = expo
            sum_ref[:, strip] = sum_ref[:, strip] + jnp.sum(expo.reshape(BLK // 8, 8, STRIP), axis=0)
            acc_ref[:, strip] = acc_ref[:, strip] + dot(value_t, expo.astype(jnp.bfloat16))
        return carry

    lax.fori_loop(0, used, output_pass, 0)
    for strip in STRIPS:
        inverse = 1.0 / jnp.sum(sum_ref[:, strip], axis=0, keepdims=True)
        out_t = (acc_ref[:, strip] * inverse).astype(jnp.bfloat16)
        delta = jnp.sum(turned(strip).astype(jnp.float32) * out_t.astype(jnp.float32), axis=0, keepdims=True)
        top_ref[:1, strip] = inverse
        sum_ref[:1, strip] = delta
        out_ref[:, strip] = out_t

    def gradient_pass(s, carry):
        value = keys_of(kv_ref, s, 1)
        key_sum = jnp.zeros((BLK, HD), jnp.float32)
        value_sum = jnp.zeros((BLK, HD), jnp.float32)
        for strip in STRIPS:
            dprob = dot(value, turned(strip))
            weights = e_ref[s, :, strip] * top_ref[:1, strip]
            dlogit = (weights * (dprob - sum_ref[:1, strip])).astype(jnp.bfloat16)
            value_sum = value_sum + dot(weights.astype(jnp.bfloat16), stacked(1, strip))
            key_sum = key_sum + dot(dlogit, stacked(0, strip))
            dl_ref[s, :, strip] = dlogit
        for kind, total in ((0, key_sum * SCALE), (1, value_sum)):
            total = total.astype(jnp.bfloat16)
            for quad in range(QUADS):
                first = pl.multiple_of(((2 * quad + kind) * ANC + s) * SHARE, SHARE)
                kvg_ref[pl.ds(first, SHARE), :] = total[quad * SHARE : (quad + 1) * SHARE]
        return carry

    lax.fori_loop(0, used, gradient_pass, 0)

def late_kernel(anc_ref, kv_ref, dl_ref, out_t_ref, out_ref, qg_ref, acc_ref):
    used = used_slots(anc_ref, anc_ref[ANC + 1, 0])
    for h in range(GROUP):
        here = slice(h * BLK, (h + 1) * BLK)
        out_ref[:, here] = out_t_ref[:, here].T
    acc_ref[...] = jnp.zeros_like(acc_ref)

    def query_pass(s, carry):
        key_t = keys_of(kv_ref, s, 0).T
        for strip in STRIPS:
            acc_ref[:, strip] = acc_ref[:, strip] + dot(key_t, dl_ref[s, :, strip])
        return carry

    lax.fori_loop(0, used, query_pass, 0)
    for h in range(GROUP):
        here = slice(h * BLK, (h + 1) * BLK)
        qg_ref[:, here] = (acc_ref[:, here] * SCALE).T


def near_memory(x):
    return pltpu.with_memory_space_constraint(x, pltpu.VMEM)


def far_memory(x):
    return pltpu.with_memory_space_constraint(x, pltpu.HBM)


SMEM = pl.BlockSpec(memory_space=pltpu.SMEM)
VMEM = pl.BlockSpec(memory_space=pltpu.VMEM)


ANY = pl.BlockSpec(memory_space=pl.ANY)
HBM = pl.BlockSpec(memory_space=pltpu.HBM)


def room(mebibytes):
    return pltpu.CompilerParams(vmem_limit_bytes=mebibytes << 20)


def shaped(shape, dtype):
    return jax.ShapeDtypeStruct(shape, dtype)


def per_device(query_in, key_in, value_in, out_grad, ancestry, node_len):
    everyone = ("far", "near", "head")
    leaf = (lax.axis_index("far") * NEAR + lax.axis_index("near")).astype(jnp.int32).reshape(1)
    ancestry_t, node_len = far_memory(ancestry.T), far_memory(node_len)
    rows = key_in.shape[0]

    low, wide = jnp.bfloat16, jnp.float32
    pieces = pl.pallas_call(
        cut_kernel,
        out_shape=pltpu.VMEM((FAR * NEAR * SHARE, HD), low),
        in_specs=[HBM, HBM],
        out_specs=VMEM,
        scratch_shapes=[
            pltpu.VMEM(key_in.shape, low),
            pltpu.VMEM(key_in.shape, low),
            pltpu.SemaphoreType.DMA((2,)),
        ],
        compiler_params=room(4),
        name="cut",
    )(far_memory(key_in), far_memory(value_in))
    table = pl.pallas_call(
        table_kernel,
        out_shape=pltpu.SMEM((2 * ANC, NODES), jnp.int32),
        in_specs=[SMEM, SMEM, SMEM],
        out_specs=SMEM,
        compiler_params=room(1),
        name="table",
    )(leaf, ancestry_t, node_len)
    shares = lax.all_to_all(pieces, everyone, split_axis=0, concat_axis=0, tiled=True)
    stacked = pl.pallas_call(
        prep_kernel,
        out_shape=pltpu.VMEM((3 * WIDE, HD), low),
        in_specs=[VMEM, VMEM],
        out_specs=VMEM,
        compiler_params=room(4),
        name="prep",
    )(query_in, out_grad)
    shares, stacked, table = lax.optimization_barrier((shares, stacked, table))
    table = pltpu.with_memory_space_constraint(table, pltpu.SMEM)
    picked = pl.pallas_call(
        pick_kernel,
        out_shape=pltpu.VMEM((NEAR * ANC * SHARE, HD), low),
        in_specs=[SMEM, VMEM],
        out_specs=VMEM,
        scratch_shapes=[pltpu.SemaphoreType.DMA((ANC,))],
        compiler_params=room(4),
        name="pick",
    )(table, near_memory(shares))
    kv = near_memory(lax.all_to_all(picked, "near", split_axis=0, concat_axis=0, tiled=True))
    terms, dlogit, out_t = pl.pallas_call(
        attention_kernel,
        out_shape=(
            pltpu.VMEM((2 * ANC * BLK, HD), low),
            pltpu.VMEM((ANC, BLK, WIDE), low),
            pltpu.VMEM((HD, WIDE), low),
        ),
        in_specs=[SMEM, VMEM, VMEM],
        out_specs=(VMEM, VMEM, VMEM),
        scratch_shapes=[
            pltpu.VMEM((ANC, BLK, WIDE), wide),
            pltpu.VMEM((8, WIDE), wide),
            pltpu.VMEM((8, WIDE), wide),
            pltpu.VMEM((HD, WIDE), wide),
        ],
        compiler_params=room(16),
        name="attend",
    )(table, near_memory(stacked), kv)
    terms = lax.all_to_all(terms, "near", split_axis=0, concat_axis=0, tiled=True)
    attended, query_grad = pl.pallas_call(
        late_kernel,
        out_shape=(shaped((BLK, GROUP * HD), low), shaped((BLK, GROUP * HD), wide)),
        in_specs=[SMEM, VMEM, VMEM, VMEM],
        out_specs=(VMEM, VMEM),
        scratch_shapes=[pltpu.VMEM((HD, WIDE), wide)],
        compiler_params=room(8),
        name="late",
    )(table, kv, near_memory(dlogit), near_memory(out_t))
    summed = pl.pallas_call(
        add_kernel,
        out_shape=pltpu.VMEM((NODES * SHARE, HD), low),
        in_specs=[SMEM, VMEM],
        out_specs=VMEM,
        scratch_shapes=[
            pltpu.VMEM(((NODES + 1) * SHARE, HD), wide),
            pltpu.VMEM(((NODES + 1) * SHARE, HD), wide),
        ],
        compiler_params=room(8),
        name="add",
    )(table, near_memory(terms))
    back = lax.all_to_all(summed, everyone, split_axis=0, concat_axis=0, tiled=True)
    key_grad, value_grad = pl.pallas_call(
        finish_kernel,
        out_shape=(shaped((rows, KVH * HD), wide), shaped((rows, KVH * HD), wide)),
        in_specs=[VMEM],
        out_specs=(VMEM, VMEM),
        compiler_params=room(8),
        name="finish",
    )(near_memory(back))
    return (attended, query_grad, key_grad, value_grad)


def solution(mesh):
    mesh = Mesh(mesh.devices.reshape(FAR, NEAR, KVH), ("far", "near", "head"))
    leaf = ("far", "near")
    token = ("far", "near", "head")
    return jax.shard_map(
        per_device,
        mesh=mesh,
        in_specs=(P(leaf, "head"), P(token, None), P(token, None), P(leaf, "head"), P(), P()),
        out_specs=(P(leaf, "head"), P(leaf, "head"), P(token, None), P(token, None)),
        check_vma=False,
    )
```

```python
import jax
import jax.numpy as jnp
from jax import lax
from jax.experimental import pallas as pl
from jax.experimental.pallas import tpu as pltpu
from jax.sharding import Mesh, PartitionSpec as P

QH = 64
KVH = 8
HD = 128
BLK = 128
ANC = 8
NODES = 32
GROUP = QH // KVH
FAR = 4
NEAR = 8
PIECE = 4
SHARE = KVH * PIECE
QUADS = 16 // PIECE
WIDE = GROUP * BLK
STRIP = 256
LOG2E = 1.4426950408889634
SCALE = HD ** (-0.5)
LOW = -1e30

NT = (((1,), (1,)), ((), ()))
NN = (((1,), (0,)), ((), ()))


def dot(a, b, dims=NN):
    return lax.dot_general(a, b, dims, preferred_element_type=jnp.float32)


def cut_kernel(key_hbm, value_hbm, out_ref, key_ref, value_ref, sems):
    kinds = ((key_hbm, key_ref), (value_hbm, value_ref))
    for kind, (far_ref, ref) in enumerate(kinds):
        pltpu.make_async_copy(far_ref, ref, sems.at[kind]).start()
    for kind, (far_ref, ref) in enumerate(kinds):
        pltpu.make_async_copy(far_ref, ref, sems.at[kind]).wait()
        rows = ref[...].astype(jnp.float32)
        for quad in range(QUADS):
            part = rows[quad * PIECE : (quad + 1) * PIECE]
            share = jnp.concatenate([part[:, h * HD : (h + 1) * HD] for h in range(KVH)], axis=0)
            share = share.astype(jnp.bfloat16)
            for f in range(FAR):
                first = (f * NEAR + quad * 2 + kind) * SHARE
                out_ref[first : first + SHARE, :] = share


def table_kernel(leaf_ref, anc_ref, len_ref, out_ref):
    for n in range(NODES):
        for a in range(ANC):
            out_ref[a, n] = anc_ref[a, n]
        out_ref[ANC, n] = len_ref[n]
    out_ref[ANC + 1, 0] = leaf_ref[0]


def prep_kernel(q_ref, g_ref, out_ref):
    for h in range(GROUP):
        here = slice(h * HD, (h + 1) * HD)
        g = g_ref[:, here]
        for part, block in enumerate((q_ref[:, here], g, g.T)):
            first = part * WIDE + h * BLK
            out_ref[first : first + BLK, :] = block


def levels_of(anc_ref):
    base = (anc_ref[ANC + 1, 0] // NEAR) * NEAR
    for s in range(ANC):
        nodes = [anc_ref[s, base + j] for j in range(NEAR)]
        highest = nodes[0]
        for node in nodes[1:]:
            highest = jnp.maximum(highest, node)
        yield s, nodes, highest >= 0


def pick_kernel(anc_ref, rows_ref, out_ref, sems):
    levels = list(levels_of(anc_ref))
    for s, nodes, some in levels:

        @pl.when(some)
        def _():
            for j, node in enumerate(nodes):
                first = pl.multiple_of(jnp.maximum(node, 0) * SHARE, SHARE)
                to = out_ref.at[pl.ds((j * ANC + s) * SHARE, SHARE), :]
                pltpu.make_async_copy(rows_ref.at[pl.ds(first, SHARE), :], to, sems.at[s]).start()

    for s, nodes, some in levels:

        @pl.when(some)
        def _():
            block = out_ref.at[: NEAR * SHARE, :]
            pltpu.make_async_copy(block, block, sems.at[s]).wait()


def add_kernel(anc_ref, terms_ref, out_ref, even_ref, odd_ref):
    def term(j, s):
        first = (j * ANC + s) * SHARE
        return terms_ref[first : first + SHARE, :].astype(jnp.float32)

    root = term(0, 0)
    for j in range(1, NEAR):
        root = root + term(j, 0)
    even_ref[:SHARE, :] = root
    even_ref[SHARE:, :] = jnp.zeros_like(even_ref[SHARE:, :])
    odd_ref[...] = jnp.zeros_like(odd_ref)
    for s, nodes, some in levels_of(anc_ref):
        if s == 0:
            continue

        @pl.when(some)
        def _():
            for j, node in enumerate(nodes):
                ref = odd_ref if j % 2 else even_ref
                place = jnp.where(node >= 0, node, NODES)
                here = pl.ds(pl.multiple_of(place * SHARE, SHARE), SHARE)
                ref[here, :] = ref[here, :] + term(j, s)

    rows = NODES * SHARE
    out_ref[...] = (even_ref[:rows, :] + odd_ref[:rows, :]).astype(jnp.bfloat16)


def finish_kernel(back_ref, key_ref, value_ref):
    part = NEAR * SHARE
    total = back_ref[:part, :].astype(jnp.float32)
    for f in range(1, FAR):
        total = total + back_ref[f * part : (f + 1) * part, :].astype(jnp.float32)
    for kind, ref in ((0, key_ref), (1, value_ref)):
        for h in range(KVH):
            rows = []
            for quad in range(QUADS):
                first = (quad * 2 + kind) * SHARE + h * PIECE
                rows.append(total[first : first + PIECE])
            ref[:, h * HD : (h + 1) * HD] = jnp.concatenate(rows, axis=0)


def keys_of(kv_ref, s, slots, kind):
    wide = slots * SHARE
    firsts = [((2 * quad + kind) * ANC + s) * SHARE for quad in range(QUADS)]
    return jnp.concatenate([kv_ref[pl.ds(pl.multiple_of(f, wide), wide), :] for f in firsts], axis=0)


def rows_of(s, slots):
    return pl.ds(pl.multiple_of(s * BLK, slots * BLK), slots * BLK)


def over_slots(used, turn):
    def both(pair, carry):
        turn(2 * pair, 2)
        return carry

    lax.fori_loop(0, used // 2, both, 0)

    @pl.when(used % 2 == 1)
    def _():
        turn(used - 1, 1)


def used_slots(anc_ref, leaf):
    used = jnp.int32(0)
    for s in range(ANC):
        used = used + jnp.where(anc_ref[s, leaf] >= 0, 1, 0)
    return used


STRIPS = [slice(i * STRIP, (i + 1) * STRIP) for i in range(WIDE // STRIP)]


def attention_kernel(
    anc_ref, in_ref, kv_ref, kvg_ref, dl_ref, out_ref,
    e_ref, p_ref, top_ref, sum_ref, acc_ref,
):
    leaf = anc_ref[ANC + 1, 0]
    used = used_slots(anc_ref, leaf)

    def stacked(part, strip):
        return in_ref[part * WIDE + strip.start : part * WIDE + strip.stop, :]

    def turned(strip):
        rows = stacked(2, strip)
        return jnp.concatenate([rows[i * HD : (i + 1) * HD] for i in range(STRIP // BLK)], axis=1)

    top_ref[...] = jnp.full_like(top_ref, LOW)
    sum_ref[...] = jnp.zeros_like(sum_ref)
    acc_ref[...] = jnp.zeros_like(acc_ref)

    def ends_of(s, query):
        node = anc_ref[s, leaf]
        length = anc_ref[ANC, node]
        return jnp.where(node == leaf, jnp.minimum(query + 1, length), length)

    def logits_turn(s, slots):
        shape = (slots * BLK, BLK)
        row = lax.broadcasted_iota(jnp.int32, shape, 0)
        query = lax.broadcasted_iota(jnp.int32, shape, 1)
        place = ((row // PIECE) % KVH) * 16 + (row // (slots * SHARE)) * PIECE + row % PIECE
        ends = ends_of(s, query)
        if slots == 2:
            ends = jnp.where((row // SHARE) % 2 == 1, ends_of(s + 1, query), ends)
        seen = jnp.concatenate([place < ends] * (STRIP // BLK), axis=1)
        key = keys_of(kv_ref, s, slots, 0)
        for strip in STRIPS:
            raw = dot(key, stacked(0, strip), NT) * (SCALE * LOG2E)
            raw = jnp.where(seen, raw, LOW)
            e_ref[rows_of(s, slots), strip] = raw
            high = jnp.max(raw.reshape(slots * BLK // 8, 8, STRIP), axis=0)
            top_ref[:, strip] = jnp.maximum(top_ref[:, strip], high)

    over_slots(used, logits_turn)
    top_ref[...] = jnp.broadcast_to(jnp.max(top_ref[...], axis=0, keepdims=True), top_ref.shape)

    def output_turn(s, slots):
        value_t = keys_of(kv_ref, s, slots, 1).T
        for strip in STRIPS:
            expo = jnp.exp2(e_ref[rows_of(s, slots), strip] - top_ref[:1, strip])
            part = jnp.sum(expo.reshape(slots * BLK // 8, 8, STRIP), axis=0)
            sum_ref[:, strip] = sum_ref[:, strip] + part
            acc_ref[:, strip] = acc_ref[:, strip] + dot(value_t, expo.astype(jnp.bfloat16))

    over_slots(used, output_turn)
    for strip in STRIPS:
        total = jnp.sum(sum_ref[:, strip], axis=0, keepdims=True)
        out_t = (acc_ref[:, strip] * (1.0 / total)).astype(jnp.bfloat16)
        delta = jnp.sum(turned(strip).astype(jnp.float32) * out_t.astype(jnp.float32), axis=0, keepdims=True)
        top_ref[:1, strip] = top_ref[:1, strip] + jnp.log2(total)
        sum_ref[:1, strip] = delta
        out_ref[:, strip] = out_t

    def gradient_turn(s, slots):
        value = keys_of(kv_ref, s, slots, 1)
        for strip in STRIPS:
            dprob = dot(value, turned(strip))
            weights = jnp.exp2(e_ref[rows_of(s, slots), strip] - top_ref[:1, strip])
            dl_ref[rows_of(s, slots), strip] = (weights * (dprob - sum_ref[:1, strip])).astype(jnp.bfloat16)
            p_ref[: slots * BLK, strip] = weights.astype(jnp.bfloat16)
        key_sum = dot(dl_ref[rows_of(s, slots), :], in_ref[:WIDE, :]) * SCALE
        value_sum = dot(p_ref[: slots * BLK, :], in_ref[WIDE : 2 * WIDE, :])
        wide = slots * SHARE
        for kind, total in ((0, key_sum), (1, value_sum)):
            total = total.astype(jnp.bfloat16)
            for quad in range(QUADS):
                first = pl.multiple_of(((2 * quad + kind) * ANC + s) * SHARE, wide)
                kvg_ref[pl.ds(first, wide), :] = total[quad * wide : (quad + 1) * wide]

    over_slots(used, gradient_turn)


def late_kernel(anc_ref, kv_ref, dl_ref, out_t_ref, out_ref, qg_ref, acc_ref):
    used = used_slots(anc_ref, anc_ref[ANC + 1, 0])
    for h in range(GROUP):
        here = slice(h * BLK, (h + 1) * BLK)
        out_ref[:, here] = out_t_ref[:, here].T
    acc_ref[...] = jnp.zeros_like(acc_ref)

    def query_turn(s, slots):
        key_t = keys_of(kv_ref, s, slots, 0).T
        for strip in STRIPS:
            acc_ref[:, strip] = acc_ref[:, strip] + dot(key_t, dl_ref[rows_of(s, slots), strip])

    over_slots(used, query_turn)
    for h in range(GROUP):
        here = slice(h * BLK, (h + 1) * BLK)
        qg_ref[:, here] = (acc_ref[:, here] * SCALE).T


def near_memory(x):
    return pltpu.with_memory_space_constraint(x, pltpu.VMEM)


def far_memory(x):
    return pltpu.with_memory_space_constraint(x, pltpu.HBM)


SMEM = pl.BlockSpec(memory_space=pltpu.SMEM)
VMEM = pl.BlockSpec(memory_space=pltpu.VMEM)


ANY = pl.BlockSpec(memory_space=pl.ANY)
HBM = pl.BlockSpec(memory_space=pltpu.HBM)


def room(mebibytes):
    return pltpu.CompilerParams(vmem_limit_bytes=mebibytes << 20)


def shaped(shape, dtype):
    return jax.ShapeDtypeStruct(shape, dtype)


def per_device(query_in, key_in, value_in, out_grad, ancestry, node_len):
    everyone = ("far", "near", "head")
    leaf = (lax.axis_index("far") * NEAR + lax.axis_index("near")).astype(jnp.int32).reshape(1)
    ancestry_t, node_len = far_memory(ancestry.T), far_memory(node_len)
    rows = key_in.shape[0]

    low, wide = jnp.bfloat16, jnp.float32
    pieces = pl.pallas_call(
        cut_kernel,
        out_shape=pltpu.VMEM((FAR * NEAR * SHARE, HD), low),
        in_specs=[HBM, HBM],
        out_specs=VMEM,
        scratch_shapes=[
            pltpu.VMEM(key_in.shape, low),
            pltpu.VMEM(key_in.shape, low),
            pltpu.SemaphoreType.DMA((2,)),
        ],
        compiler_params=room(4),
        name="cut",
    )(far_memory(key_in), far_memory(value_in))
    table = pl.pallas_call(
        table_kernel,
        out_shape=pltpu.SMEM((2 * ANC, NODES), jnp.int32),
        in_specs=[SMEM, SMEM, SMEM],
        out_specs=SMEM,
        compiler_params=room(1),
        name="table",
    )(leaf, ancestry_t, node_len)
    shares = lax.all_to_all(pieces, everyone, split_axis=0, concat_axis=0, tiled=True)
    stacked = pl.pallas_call(
        prep_kernel,
        out_shape=pltpu.VMEM((3 * WIDE, HD), low),
        in_specs=[VMEM, VMEM],
        out_specs=VMEM,
        compiler_params=room(4),
        name="prep",
    )(query_in, out_grad)
    shares, stacked, table = lax.optimization_barrier((shares, stacked, table))
    table = pltpu.with_memory_space_constraint(table, pltpu.SMEM)
    picked = pl.pallas_call(
        pick_kernel,
        out_shape=pltpu.VMEM((NEAR * ANC * SHARE, HD), low),
        in_specs=[SMEM, VMEM],
        out_specs=VMEM,
        scratch_shapes=[pltpu.SemaphoreType.DMA((ANC,))],
        compiler_params=room(4),
        name="pick",
    )(table, near_memory(shares))
    kv = near_memory(lax.all_to_all(picked, "near", split_axis=0, concat_axis=0, tiled=True))
    terms, dlogit, out_t = pl.pallas_call(
        attention_kernel,
        out_shape=(
            pltpu.VMEM((2 * ANC * BLK, HD), low),
            pltpu.VMEM((ANC * BLK, WIDE), low),
            pltpu.VMEM((HD, WIDE), low),
        ),
        in_specs=[SMEM, VMEM, VMEM],
        out_specs=(VMEM, VMEM, VMEM),
        scratch_shapes=[
            pltpu.VMEM((ANC * BLK, WIDE), wide),
            pltpu.VMEM((2 * BLK, WIDE), low),
            pltpu.VMEM((8, WIDE), wide),
            pltpu.VMEM((8, WIDE), wide),
            pltpu.VMEM((HD, WIDE), wide),
        ],
        compiler_params=room(16),
        name="attend",
    )(table, near_memory(stacked), kv)
    terms = lax.all_to_all(terms, "near", split_axis=0, concat_axis=0, tiled=True)
    attended, query_grad = pl.pallas_call(
        late_kernel,
        out_shape=(shaped((BLK, GROUP * HD), low), shaped((BLK, GROUP * HD), wide)),
        in_specs=[SMEM, VMEM, VMEM, VMEM],
        out_specs=(VMEM, VMEM),
        scratch_shapes=[pltpu.VMEM((HD, WIDE), wide)],
        compiler_params=room(8),
        name="late",
    )(table, kv, near_memory(dlogit), near_memory(out_t))
    summed = pl.pallas_call(
        add_kernel,
        out_shape=pltpu.VMEM((NODES * SHARE, HD), low),
        in_specs=[SMEM, VMEM],
        out_specs=VMEM,
        scratch_shapes=[
            pltpu.VMEM(((NODES + 1) * SHARE, HD), wide),
            pltpu.VMEM(((NODES + 1) * SHARE, HD), wide),
        ],
        compiler_params=room(8),
        name="add",
    )(table, near_memory(terms))
    back = lax.all_to_all(summed, everyone, split_axis=0, concat_axis=0, tiled=True)
    key_grad, value_grad = pl.pallas_call(
        finish_kernel,
        out_shape=(shaped((rows, KVH * HD), wide), shaped((rows, KVH * HD), wide)),
        in_specs=[VMEM],
        out_specs=(VMEM, VMEM),
        compiler_params=room(8),
        name="finish",
    )(near_memory(back))
    return (attended, query_grad, key_grad, value_grad)


def solution(mesh):
    mesh = Mesh(mesh.devices.reshape(FAR, NEAR, KVH), ("far", "near", "head"))
    leaf = ("far", "near")
    token = ("far", "near", "head")
    return jax.shard_map(
        per_device,
        mesh=mesh,
        in_specs=(P(leaf, "head"), P(token, None), P(token, None), P(leaf, "head"), P(), P()),
        out_specs=(P(leaf, "head"), P(leaf, "head"), P(token, None), P(token, None)),
        check_vma=False,
    )
```

```python
import jax
import jax.numpy as jnp
from jax import lax
from jax.experimental import pallas as pl
from jax.experimental.pallas import tpu as pltpu
from jax.sharding import Mesh, PartitionSpec as P

QH = 64
KVH = 8
HD = 128
BLK = 128
ANC = 8
NODES = 32
GROUP = QH // KVH
FAR = 4
NEAR = 8
PIECE = 4
SHARE = KVH * PIECE
QUADS = 16 // PIECE
WIDE = GROUP * BLK
STRIP = 256
LOG2E = 1.4426950408889634
SCALE = HD ** (-0.5)
LOW = -1e30

NT = (((1,), (1,)), ((), ()))
NN = (((1,), (0,)), ((), ()))


def dot(a, b, dims=NN):
    return lax.dot_general(a, b, dims, preferred_element_type=jnp.float32)


def cut_kernel(key_hbm, value_hbm, out_ref, key_ref, value_ref, sems):
    kinds = ((key_hbm, key_ref), (value_hbm, value_ref))
    for kind, (far_ref, ref) in enumerate(kinds):
        pltpu.make_async_copy(far_ref, ref, sems.at[kind]).start()
    for kind, (far_ref, ref) in enumerate(kinds):
        pltpu.make_async_copy(far_ref, ref, sems.at[kind]).wait()
        rows = ref[...].astype(jnp.float32)
        for quad in range(QUADS):
            part = rows[quad * PIECE : (quad + 1) * PIECE]
            share = jnp.concatenate([part[:, h * HD : (h + 1) * HD] for h in range(KVH)], axis=0)
            share = share.astype(jnp.bfloat16)
            for f in range(FAR):
                first = (f * NEAR + quad * 2 + kind) * SHARE
                out_ref[first : first + SHARE, :] = share


def table_kernel(leaf_ref, anc_ref, len_ref, out_ref):
    for n in range(NODES):
        for a in range(ANC):
            out_ref[a, n] = anc_ref[a, n]
        out_ref[ANC, n] = len_ref[n]
    out_ref[ANC + 1, 0] = leaf_ref[0]


def prep_kernel(q_ref, g_ref, out_ref):
    for h in range(GROUP):
        here = slice(h * HD, (h + 1) * HD)
        g = g_ref[:, here]
        for part, block in enumerate((q_ref[:, here], g, g.T)):
            first = part * WIDE + h * BLK
            out_ref[first : first + BLK, :] = block


def levels_of(anc_ref):
    base = (anc_ref[ANC + 1, 0] // NEAR) * NEAR
    for s in range(ANC):
        nodes = [anc_ref[s, base + j] for j in range(NEAR)]
        highest = nodes[0]
        for node in nodes[1:]:
            highest = jnp.maximum(highest, node)
        yield s, nodes, highest >= 0


def pick_kernel(anc_ref, rows_ref, out_ref, sems):
    levels = list(levels_of(anc_ref))
    for s, nodes, some in levels:

        @pl.when(some)
        def _():
            for j, node in enumerate(nodes):
                first = pl.multiple_of(jnp.maximum(node, 0) * SHARE, SHARE)
                to = out_ref.at[pl.ds((j * ANC + s) * SHARE, SHARE), :]
                pltpu.make_async_copy(rows_ref.at[pl.ds(first, SHARE), :], to, sems.at[s]).start()

    for s, nodes, some in levels:

        @pl.when(some)
        def _():
            block = out_ref.at[: NEAR * SHARE, :]
            pltpu.make_async_copy(block, block, sems.at[s]).wait()


def add_kernel(anc_ref, terms_ref, out_ref, even_ref, odd_ref):
    def term(j, s):
        first = (j * ANC + s) * SHARE
        return terms_ref[first : first + SHARE, :].astype(jnp.float32)

    root = term(0, 0)
    for j in range(1, NEAR):
        root = root + term(j, 0)
    even_ref[:SHARE, :] = root
    even_ref[SHARE:, :] = jnp.zeros_like(even_ref[SHARE:, :])
    odd_ref[...] = jnp.zeros_like(odd_ref)
    for s, nodes, some in levels_of(anc_ref):
        if s == 0:
            continue

        @pl.when(some)
        def _():
            for j, node in enumerate(nodes):
                ref = odd_ref if j % 2 else even_ref
                place = jnp.where(node >= 0, node, NODES)
                here = pl.ds(pl.multiple_of(place * SHARE, SHARE), SHARE)
                ref[here, :] = ref[here, :] + term(j, s)

    rows = NODES * SHARE
    out_ref[...] = (even_ref[:rows, :] + odd_ref[:rows, :]).astype(jnp.bfloat16)


def finish_kernel(back_ref, key_ref, value_ref):
    part = NEAR * SHARE
    total = back_ref[:part, :].astype(jnp.float32)
    for f in range(1, FAR):
        total = total + back_ref[f * part : (f + 1) * part, :].astype(jnp.float32)
    for kind, ref in ((0, key_ref), (1, value_ref)):
        for h in range(KVH):
            rows = []
            for quad in range(QUADS):
                first = (quad * 2 + kind) * SHARE + h * PIECE
                rows.append(total[first : first + PIECE])
            ref[:, h * HD : (h + 1) * HD] = jnp.concatenate(rows, axis=0)


def keys_of(kv_ref, s, slots, kind):
    wide = slots * SHARE
    firsts = [((2 * quad + kind) * ANC + s) * SHARE for quad in range(QUADS)]
    return jnp.concatenate([kv_ref[pl.ds(pl.multiple_of(f, wide), wide), :] for f in firsts], axis=0)


def rows_of(s, slots):
    return pl.ds(pl.multiple_of(s * BLK, slots * BLK), slots * BLK)


def over_slots(used, turn):
    def both(pair, carry):
        turn(2 * pair, 2)
        return carry

    lax.fori_loop(0, used // 2, both, 0)

    @pl.when(used % 2 == 1)
    def _():
        turn(used - 1, 1)


def used_slots(anc_ref, leaf):
    used = jnp.int32(0)
    for s in range(ANC):
        used = used + jnp.where(anc_ref[s, leaf] >= 0, 1, 0)
    return used


STRIPS = [slice(i * STRIP, (i + 1) * STRIP) for i in range(WIDE // STRIP)]


def attention_kernel(
    anc_ref, in_ref, kv_ref, kvg_ref, dl_ref, out_ref,
    e_ref, p_ref, top_ref, sum_ref, acc_ref,
):
    leaf = anc_ref[ANC + 1, 0]
    used = used_slots(anc_ref, leaf)

    def stacked(part, strip):
        return in_ref[part * WIDE + strip.start : part * WIDE + strip.stop, :]

    def turned(strip):
        rows = stacked(2, strip)
        return jnp.concatenate([rows[i * HD : (i + 1) * HD] for i in range(STRIP // BLK)], axis=1)

    top_ref[...] = jnp.full_like(top_ref, LOW)
    sum_ref[...] = jnp.zeros_like(sum_ref)
    acc_ref[...] = jnp.zeros_like(acc_ref)

    block = lax.broadcasted_iota(jnp.int32, (8, BLK), 0)
    inside = (block // PIECE) * 16 + block % PIECE
    query = lax.broadcasted_iota(jnp.int32, (8, BLK), 1)

    def room_of(s):
        node = anc_ref[s, leaf]
        length = anc_ref[ANC, node]
        return jnp.where(node == leaf, jnp.minimum(query + 1, length), length) - inside

    def logits_turn(s, slots):
        ends = [room_of(s + i) for i in range(slots)]
        left = [
            ends[i] - (quad * PIECE + pair * 32)
            for quad in range(QUADS)
            for i in range(slots)
            for pair in range(SHARE // 8)
        ]
        seen = jnp.concatenate(left, axis=0) > 0
        seen = jnp.concatenate([seen] * (STRIP // BLK), axis=1)
        key = keys_of(kv_ref, s, slots, 0)
        for strip in STRIPS:
            raw = dot(key, stacked(0, strip), NT) * (SCALE * LOG2E)
            raw = jnp.where(seen, raw, LOW)
            e_ref[rows_of(s, slots), strip] = raw
            high = jnp.max(raw.reshape(slots * BLK // 8, 8, STRIP), axis=0)
            top_ref[:, strip] = jnp.maximum(top_ref[:, strip], high)

    over_slots(used, logits_turn)
    top_ref[...] = jnp.broadcast_to(jnp.max(top_ref[...], axis=0, keepdims=True), top_ref.shape)

    def output_turn(s, slots):
        value_t = keys_of(kv_ref, s, slots, 1).T
        for strip in STRIPS:
            expo = jnp.exp2(e_ref[rows_of(s, slots), strip] - top_ref[:1, strip])
            part = jnp.sum(expo.reshape(slots * BLK // 8, 8, STRIP), axis=0)
            sum_ref[:, strip] = sum_ref[:, strip] + part
            acc_ref[:, strip] = acc_ref[:, strip] + dot(value_t, expo.astype(jnp.bfloat16))

    over_slots(used, output_turn)
    for strip in STRIPS:
        total = jnp.sum(sum_ref[:, strip], axis=0, keepdims=True)
        out_t = (acc_ref[:, strip] * (1.0 / total)).astype(jnp.bfloat16)
        delta = jnp.sum(turned(strip).astype(jnp.float32) * out_t.astype(jnp.float32), axis=0, keepdims=True)
        top_ref[:1, strip] = top_ref[:1, strip] + jnp.log2(total)
        sum_ref[:1, strip] = delta
        out_ref[:, strip] = out_t

    def gradient_turn(s, slots):
        value = keys_of(kv_ref, s, slots, 1)
        for strip in STRIPS:
            dprob = dot(value, turned(strip))
            weights = jnp.exp2(e_ref[rows_of(s, slots), strip] - top_ref[:1, strip])
            dl_ref[rows_of(s, slots), strip] = (weights * (dprob - sum_ref[:1, strip])).astype(jnp.bfloat16)
            p_ref[: slots * BLK, strip] = weights.astype(jnp.bfloat16)
        key_sum = dot(dl_ref[rows_of(s, slots), :], in_ref[:WIDE, :]) * SCALE
        value_sum = dot(p_ref[: slots * BLK, :], in_ref[WIDE : 2 * WIDE, :])
        wide = slots * SHARE
        for kind, total in ((0, key_sum), (1, value_sum)):
            total = total.astype(jnp.bfloat16)
            for quad in range(QUADS):
                first = pl.multiple_of(((2 * quad + kind) * ANC + s) * SHARE, wide)
                kvg_ref[pl.ds(first, wide), :] = total[quad * wide : (quad + 1) * wide]

    over_slots(used, gradient_turn)


def late_kernel(anc_ref, kv_ref, dl_ref, out_t_ref, out_ref, qg_ref, acc_ref):
    used = used_slots(anc_ref, anc_ref[ANC + 1, 0])
    for h in range(GROUP):
        here = slice(h * BLK, (h + 1) * BLK)
        out_ref[:, here] = out_t_ref[:, here].T
    acc_ref[...] = jnp.zeros_like(acc_ref)

    def query_turn(s, slots):
        key_t = keys_of(kv_ref, s, slots, 0).T
        for strip in STRIPS:
            acc_ref[:, strip] = acc_ref[:, strip] + dot(key_t, dl_ref[rows_of(s, slots), strip])

    over_slots(used, query_turn)
    for h in range(GROUP):
        here = slice(h * BLK, (h + 1) * BLK)
        qg_ref[:, here] = (acc_ref[:, here] * SCALE).T


def near_memory(x):
    return pltpu.with_memory_space_constraint(x, pltpu.VMEM)


def far_memory(x):
    return pltpu.with_memory_space_constraint(x, pltpu.HBM)


SMEM = pl.BlockSpec(memory_space=pltpu.SMEM)
VMEM = pl.BlockSpec(memory_space=pltpu.VMEM)


ANY = pl.BlockSpec(memory_space=pl.ANY)
HBM = pl.BlockSpec(memory_space=pltpu.HBM)


def room(mebibytes):
    return pltpu.CompilerParams(vmem_limit_bytes=mebibytes << 20)


def shaped(shape, dtype):
    return jax.ShapeDtypeStruct(shape, dtype)


def per_device(query_in, key_in, value_in, out_grad, ancestry, node_len):
    everyone = ("far", "near", "head")
    leaf = (lax.axis_index("far") * NEAR + lax.axis_index("near")).astype(jnp.int32).reshape(1)
    ancestry_t, node_len = far_memory(ancestry.T), far_memory(node_len)
    rows = key_in.shape[0]

    low, wide = jnp.bfloat16, jnp.float32
    pieces = pl.pallas_call(
        cut_kernel,
        out_shape=pltpu.VMEM((FAR * NEAR * SHARE, HD), low),
        in_specs=[HBM, HBM],
        out_specs=VMEM,
        scratch_shapes=[
            pltpu.VMEM(key_in.shape, low),
            pltpu.VMEM(key_in.shape, low),
            pltpu.SemaphoreType.DMA((2,)),
        ],
        compiler_params=room(4),
        name="cut",
    )(far_memory(key_in), far_memory(value_in))
    table = pl.pallas_call(
        table_kernel,
        out_shape=pltpu.SMEM((2 * ANC, NODES), jnp.int32),
        in_specs=[SMEM, SMEM, SMEM],
        out_specs=SMEM,
        compiler_params=room(1),
        name="table",
    )(leaf, ancestry_t, node_len)
    shares = lax.all_to_all(pieces, everyone, split_axis=0, concat_axis=0, tiled=True)
    stacked = pl.pallas_call(
        prep_kernel,
        out_shape=pltpu.VMEM((3 * WIDE, HD), low),
        in_specs=[VMEM, VMEM],
        out_specs=VMEM,
        compiler_params=room(4),
        name="prep",
    )(query_in, out_grad)
    shares, stacked, table = lax.optimization_barrier((shares, stacked, table))
    table = pltpu.with_memory_space_constraint(table, pltpu.SMEM)
    picked = pl.pallas_call(
        pick_kernel,
        out_shape=pltpu.VMEM((NEAR * ANC * SHARE, HD), low),
        in_specs=[SMEM, VMEM],
        out_specs=VMEM,
        scratch_shapes=[pltpu.SemaphoreType.DMA((ANC,))],
        compiler_params=room(4),
        name="pick",
    )(table, near_memory(shares))
    kv = near_memory(lax.all_to_all(picked, "near", split_axis=0, concat_axis=0, tiled=True))
    terms, dlogit, out_t = pl.pallas_call(
        attention_kernel,
        out_shape=(
            pltpu.VMEM((2 * ANC * BLK, HD), low),
            pltpu.VMEM((ANC * BLK, WIDE), low),
            pltpu.VMEM((HD, WIDE), low),
        ),
        in_specs=[SMEM, VMEM, VMEM],
        out_specs=(VMEM, VMEM, VMEM),
        scratch_shapes=[
            pltpu.VMEM((ANC * BLK, WIDE), wide),
            pltpu.VMEM((2 * BLK, WIDE), low),
            pltpu.VMEM((8, WIDE), wide),
            pltpu.VMEM((8, WIDE), wide),
            pltpu.VMEM((HD, WIDE), wide),
        ],
        compiler_params=room(16),
        name="attend",
    )(table, near_memory(stacked), kv)
    terms = lax.all_to_all(terms, "near", split_axis=0, concat_axis=0, tiled=True)
    attended, query_grad = pl.pallas_call(
        late_kernel,
        out_shape=(shaped((BLK, GROUP * HD), low), shaped((BLK, GROUP * HD), wide)),
        in_specs=[SMEM, VMEM, VMEM, VMEM],
        out_specs=(VMEM, VMEM),
        scratch_shapes=[pltpu.VMEM((HD, WIDE), wide)],
        compiler_params=room(8),
        name="late",
    )(table, kv, near_memory(dlogit), near_memory(out_t))
    summed = pl.pallas_call(
        add_kernel,
        out_shape=pltpu.VMEM((NODES * SHARE, HD), low),
        in_specs=[SMEM, VMEM],
        out_specs=VMEM,
        scratch_shapes=[
            pltpu.VMEM(((NODES + 1) * SHARE, HD), wide),
            pltpu.VMEM(((NODES + 1) * SHARE, HD), wide),
        ],
        compiler_params=room(8),
        name="add",
    )(table, near_memory(terms))
    back = lax.all_to_all(summed, everyone, split_axis=0, concat_axis=0, tiled=True)
    key_grad, value_grad = pl.pallas_call(
        finish_kernel,
        out_shape=(shaped((rows, KVH * HD), wide), shaped((rows, KVH * HD), wide)),
        in_specs=[VMEM],
        out_specs=(VMEM, VMEM),
        compiler_params=room(8),
        name="finish",
    )(near_memory(back))
    return (attended, query_grad, key_grad, value_grad)


def solution(mesh):
    mesh = Mesh(mesh.devices.reshape(FAR, NEAR, KVH), ("far", "near", "head"))
    leaf = ("far", "near")
    token = ("far", "near", "head")
    return jax.shard_map(
        per_device,
        mesh=mesh,
        in_specs=(P(leaf, "head"), P(token, None), P(token, None), P(leaf, "head"), P(), P()),
        out_specs=(P(leaf, "head"), P(leaf, "head"), P(token, None), P(token, None)),
        check_vma=False,
    )
```

```python
import jax
import jax.numpy as jnp
from jax import lax
from jax.experimental import pallas as pl
from jax.experimental.pallas import tpu as pltpu
from jax.sharding import Mesh, PartitionSpec as P

QH = 64
KVH = 8
HD = 128
BLK = 128
ANC = 8
NODES = 32
GROUP = QH // KVH
FAR = 4
NEAR = 8
PIECE = 4
SHARE = KVH * PIECE
QUADS = 16 // PIECE
WIDE = GROUP * BLK
STRIP = 256
LOG2E = 1.4426950408889634
SCALE = HD ** (-0.5)
LOW = -1e30

NT = (((1,), (1,)), ((), ()))
NN = (((1,), (0,)), ((), ()))


def dot(a, b, dims=NN):
    return lax.dot_general(a, b, dims, preferred_element_type=jnp.float32)


def cut_kernel(key_hbm, value_hbm, out_ref, key_ref, value_ref, sems):
    kinds = ((key_hbm, key_ref), (value_hbm, value_ref))
    for kind, (far_ref, ref) in enumerate(kinds):
        pltpu.make_async_copy(far_ref, ref, sems.at[kind]).start()
    for kind, (far_ref, ref) in enumerate(kinds):
        pltpu.make_async_copy(far_ref, ref, sems.at[kind]).wait()
        rows = ref[...].astype(jnp.float32)
        for quad in range(QUADS):
            part = rows[quad * PIECE : (quad + 1) * PIECE]
            share = jnp.concatenate([part[:, h * HD : (h + 1) * HD] for h in range(KVH)], axis=0)
            share = share.astype(jnp.bfloat16)
            for f in range(FAR):
                first = (f * NEAR + quad * 2 + kind) * SHARE
                out_ref[first : first + SHARE, :] = share


def table_kernel(leaf_ref, anc_ref, len_ref, out_ref):
    for n in range(NODES):
        for a in range(ANC):
            out_ref[a, n] = anc_ref[a, n]
        out_ref[ANC, n] = len_ref[n]
    out_ref[ANC + 1, 0] = leaf_ref[0]


def prep_kernel(q_ref, g_ref, out_ref):
    for h in range(GROUP):
        here = slice(h * HD, (h + 1) * HD)
        g = g_ref[:, here]
        for part, block in enumerate((q_ref[:, here], g, g.T)):
            first = part * WIDE + h * BLK
            out_ref[first : first + BLK, :] = block


def levels_of(anc_ref):
    base = (anc_ref[ANC + 1, 0] // NEAR) * NEAR
    for s in range(ANC):
        nodes = [anc_ref[s, base + j] for j in range(NEAR)]
        highest = nodes[0]
        for node in nodes[1:]:
            highest = jnp.maximum(highest, node)
        yield s, nodes, highest >= 0


def pick_kernel(anc_ref, rows_ref, out_ref, sems):
    levels = list(levels_of(anc_ref))
    for s, nodes, some in levels:

        @pl.when(some)
        def _():
            for j, node in enumerate(nodes):
                first = pl.multiple_of(jnp.maximum(node, 0) * SHARE, SHARE)
                to = out_ref.at[pl.ds((j * ANC + s) * SHARE, SHARE), :]
                pltpu.make_async_copy(rows_ref.at[pl.ds(first, SHARE), :], to, sems.at[s]).start()

    for s, nodes, some in levels:

        @pl.when(some)
        def _():
            block = out_ref.at[: NEAR * SHARE, :]
            pltpu.make_async_copy(block, block, sems.at[s]).wait()


def add_kernel(anc_ref, terms_ref, out_hbm, even_ref, odd_ref, out_ref, sems):
    def term(j, s):
        first = (j * ANC + s) * SHARE
        return terms_ref[first : first + SHARE, :].astype(jnp.float32)

    root = term(0, 0)
    for j in range(1, NEAR):
        root = root + term(j, 0)
    even_ref[:SHARE, :] = root
    even_ref[SHARE:, :] = jnp.zeros_like(even_ref[SHARE:, :])
    odd_ref[...] = jnp.zeros_like(odd_ref)
    for s, nodes, some in levels_of(anc_ref):
        if s == 0:
            continue

        @pl.when(some)
        def _():
            for j, node in enumerate(nodes):
                ref = odd_ref if j % 2 else even_ref
                place = jnp.where(node >= 0, node, NODES)
                here = pl.ds(pl.multiple_of(place * SHARE, SHARE), SHARE)
                ref[here, :] = ref[here, :] + term(j, s)

    part = NODES * SHARE // 4
    copies = []
    for c in range(4):
        here = slice(c * part, (c + 1) * part)
        out_ref[here, :] = (even_ref[here, :] + odd_ref[here, :]).astype(jnp.bfloat16)
        copies.append(pltpu.make_async_copy(out_ref.at[here, :], out_hbm.at[here, :], sems.at[c]))
        copies[-1].start()
    for copy in copies:
        copy.wait()


def finish_kernel(back_ref, key_ref, value_ref):
    part = NEAR * SHARE
    total = back_ref[:part, :].astype(jnp.float32)
    for f in range(1, FAR):
        total = total + back_ref[f * part : (f + 1) * part, :].astype(jnp.float32)
    for kind, ref in ((0, key_ref), (1, value_ref)):
        for h in range(KVH):
            rows = []
            for quad in range(QUADS):
                first = (quad * 2 + kind) * SHARE + h * PIECE
                rows.append(total[first : first + PIECE])
            ref[:, h * HD : (h + 1) * HD] = jnp.concatenate(rows, axis=0)


def keys_of(kv_ref, s, slots, kind):
    wide = slots * SHARE
    firsts = [((2 * quad + kind) * ANC + s) * SHARE for quad in range(QUADS)]
    return jnp.concatenate([kv_ref[pl.ds(pl.multiple_of(f, wide), wide), :] for f in firsts], axis=0)


def rows_of(s, slots):
    return pl.ds(pl.multiple_of(s * BLK, slots * BLK), slots * BLK)


def over_slots(used, turn):
    def both(pair, carry):
        turn(2 * pair, 2)
        return carry

    lax.fori_loop(0, used // 2, both, 0)

    @pl.when(used % 2 == 1)
    def _():
        turn(used - 1, 1)


def used_slots(anc_ref, leaf):
    used = jnp.int32(0)
    for s in range(ANC):
        used = used + jnp.where(anc_ref[s, leaf] >= 0, 1, 0)
    return used


STRIPS = [slice(i * STRIP, (i + 1) * STRIP) for i in range(WIDE // STRIP)]


def attention_kernel(
    anc_ref, in_ref, kv_ref, kvg_ref, dl_ref, out_ref,
    e_ref, p_ref, top_ref, sum_ref, acc_ref,
):
    leaf = anc_ref[ANC + 1, 0]
    used = used_slots(anc_ref, leaf)

    def stacked(part, strip):
        return in_ref[part * WIDE + strip.start : part * WIDE + strip.stop, :]

    def turned(strip):
        rows = stacked(2, strip)
        return jnp.concatenate([rows[i * HD : (i + 1) * HD] for i in range(STRIP // BLK)], axis=1)

    top_ref[...] = jnp.full_like(top_ref, LOW)
    sum_ref[...] = jnp.zeros_like(sum_ref)
    acc_ref[...] = jnp.zeros_like(acc_ref)

    block = lax.broadcasted_iota(jnp.int32, (8, BLK), 0)
    inside = (block // PIECE) * 16 + block % PIECE
    query = lax.broadcasted_iota(jnp.int32, (8, BLK), 1)

    def room_of(s):
        node = anc_ref[s, leaf]
        length = anc_ref[ANC, node]
        return jnp.where(node == leaf, jnp.minimum(query + 1, length), length) - inside

    def logits_turn(s, slots):
        ends = [room_of(s + i) for i in range(slots)]
        left = [
            ends[i] - (quad * PIECE + pair * 32)
            for quad in range(QUADS)
            for i in range(slots)
            for pair in range(SHARE // 8)
        ]
        seen = jnp.concatenate(left, axis=0) > 0
        seen = jnp.concatenate([seen] * (STRIP // BLK), axis=1)
        key = keys_of(kv_ref, s, slots, 0)
        for strip in STRIPS:
            raw = dot(key, stacked(0, strip), NT) * (SCALE * LOG2E)
            raw = jnp.where(seen, raw, LOW)
            e_ref[rows_of(s, slots), strip] = raw
            high = jnp.max(raw.reshape(slots * BLK // 8, 8, STRIP), axis=0)
            top_ref[:, strip] = jnp.maximum(top_ref[:, strip], high)

    over_slots(used, logits_turn)
    top_ref[...] = jnp.broadcast_to(jnp.max(top_ref[...], axis=0, keepdims=True), top_ref.shape)

    def output_turn(s, slots):
        value_t = keys_of(kv_ref, s, slots, 1).T
        for strip in STRIPS:
            expo = jnp.exp2(e_ref[rows_of(s, slots), strip] - top_ref[:1, strip])
            part = jnp.sum(expo.reshape(slots * BLK // 8, 8, STRIP), axis=0)
            sum_ref[:, strip] = sum_ref[:, strip] + part
            acc_ref[:, strip] = acc_ref[:, strip] + dot(value_t, expo.astype(jnp.bfloat16))

    over_slots(used, output_turn)
    for strip in STRIPS:
        total = jnp.sum(sum_ref[:, strip], axis=0, keepdims=True)
        out_t = (acc_ref[:, strip] * (1.0 / total)).astype(jnp.bfloat16)
        delta = jnp.sum(turned(strip).astype(jnp.float32) * out_t.astype(jnp.float32), axis=0, keepdims=True)
        top_ref[:1, strip] = top_ref[:1, strip] + jnp.log2(total)
        sum_ref[:1, strip] = delta
        out_ref[:, strip] = out_t

    def gradient_turn(s, slots):
        value = keys_of(kv_ref, s, slots, 1)
        for strip in STRIPS:
            dprob = dot(value, turned(strip))
            weights = jnp.exp2(e_ref[rows_of(s, slots), strip] - top_ref[:1, strip])
            dl_ref[rows_of(s, slots), strip] = (weights * (dprob - sum_ref[:1, strip])).astype(jnp.bfloat16)
            p_ref[: slots * BLK, strip] = weights.astype(jnp.bfloat16)
        key_sum = dot(dl_ref[rows_of(s, slots), :], in_ref[:WIDE, :]) * SCALE
        value_sum = dot(p_ref[: slots * BLK, :], in_ref[WIDE : 2 * WIDE, :])
        wide = slots * SHARE
        for kind, total in ((0, key_sum), (1, value_sum)):
            total = total.astype(jnp.bfloat16)
            for quad in range(QUADS):
                first = pl.multiple_of(((2 * quad + kind) * ANC + s) * SHARE, wide)
                kvg_ref[pl.ds(first, wide), :] = total[quad * wide : (quad + 1) * wide]

    over_slots(used, gradient_turn)


def late_kernel(anc_ref, kv_ref, dl_ref, out_t_ref, out_ref, qg_ref, acc_ref):
    used = used_slots(anc_ref, anc_ref[ANC + 1, 0])
    for h in range(GROUP):
        here = slice(h * BLK, (h + 1) * BLK)
        out_ref[:, here] = out_t_ref[:, here].T
    acc_ref[...] = jnp.zeros_like(acc_ref)

    def query_turn(s, slots):
        key_t = keys_of(kv_ref, s, slots, 0).T
        for strip in STRIPS:
            acc_ref[:, strip] = acc_ref[:, strip] + dot(key_t, dl_ref[rows_of(s, slots), strip])

    over_slots(used, query_turn)
    for h in range(GROUP):
        here = slice(h * BLK, (h + 1) * BLK)
        qg_ref[:, here] = (acc_ref[:, here] * SCALE).T


def near_memory(x):
    return pltpu.with_memory_space_constraint(x, pltpu.VMEM)


def far_memory(x):
    return pltpu.with_memory_space_constraint(x, pltpu.HBM)


SMEM = pl.BlockSpec(memory_space=pltpu.SMEM)
VMEM = pl.BlockSpec(memory_space=pltpu.VMEM)


ANY = pl.BlockSpec(memory_space=pl.ANY)
HBM = pl.BlockSpec(memory_space=pltpu.HBM)


def room(mebibytes):
    return pltpu.CompilerParams(vmem_limit_bytes=mebibytes << 20)


def shaped(shape, dtype):
    return jax.ShapeDtypeStruct(shape, dtype)


def per_device(query_in, key_in, value_in, out_grad, ancestry, node_len):
    everyone = ("far", "near", "head")
    leaf = (lax.axis_index("far") * NEAR + lax.axis_index("near")).astype(jnp.int32).reshape(1)
    ancestry_t, node_len = far_memory(ancestry.T), far_memory(node_len)
    rows = key_in.shape[0]

    low, wide = jnp.bfloat16, jnp.float32
    pieces = pl.pallas_call(
        cut_kernel,
        out_shape=pltpu.VMEM((FAR * NEAR * SHARE, HD), low),
        in_specs=[HBM, HBM],
        out_specs=VMEM,
        scratch_shapes=[
            pltpu.VMEM(key_in.shape, low),
            pltpu.VMEM(key_in.shape, low),
            pltpu.SemaphoreType.DMA((2,)),
        ],
        compiler_params=room(4),
        name="cut",
    )(far_memory(key_in), far_memory(value_in))
    table = pl.pallas_call(
        table_kernel,
        out_shape=pltpu.SMEM((2 * ANC, NODES), jnp.int32),
        in_specs=[SMEM, SMEM, SMEM],
        out_specs=SMEM,
        compiler_params=room(1),
        name="table",
    )(leaf, ancestry_t, node_len)
    shares = lax.all_to_all(pieces, everyone, split_axis=0, concat_axis=0, tiled=True)
    stacked = pl.pallas_call(
        prep_kernel,
        out_shape=pltpu.VMEM((3 * WIDE, HD), low),
        in_specs=[VMEM, VMEM],
        out_specs=VMEM,
        compiler_params=room(4),
        name="prep",
    )(query_in, out_grad)
    shares, stacked, table = lax.optimization_barrier((shares, stacked, table))
    table = pltpu.with_memory_space_constraint(table, pltpu.SMEM)
    picked = pl.pallas_call(
        pick_kernel,
        out_shape=pltpu.VMEM((NEAR * ANC * SHARE, HD), low),
        in_specs=[SMEM, VMEM],
        out_specs=VMEM,
        scratch_shapes=[pltpu.SemaphoreType.DMA((ANC,))],
        compiler_params=room(4),
        name="pick",
    )(table, near_memory(shares))
    kv = near_memory(lax.all_to_all(picked, "near", split_axis=0, concat_axis=0, tiled=True))
    terms, dlogit, out_t = pl.pallas_call(
        attention_kernel,
        out_shape=(
            pltpu.VMEM((2 * ANC * BLK, HD), low),
            pltpu.VMEM((ANC * BLK, WIDE), low),
            pltpu.VMEM((HD, WIDE), low),
        ),
        in_specs=[SMEM, VMEM, VMEM],
        out_specs=(VMEM, VMEM, VMEM),
        scratch_shapes=[
            pltpu.VMEM((ANC * BLK, WIDE), wide),
            pltpu.VMEM((2 * BLK, WIDE), low),
            pltpu.VMEM((8, WIDE), wide),
            pltpu.VMEM((8, WIDE), wide),
            pltpu.VMEM((HD, WIDE), wide),
        ],
        compiler_params=room(16),
        name="attend",
    )(table, near_memory(stacked), kv)
    terms = lax.all_to_all(terms, "near", split_axis=0, concat_axis=0, tiled=True)
    attended, query_grad = pl.pallas_call(
        late_kernel,
        out_shape=(shaped((BLK, GROUP * HD), low), shaped((BLK, GROUP * HD), wide)),
        in_specs=[SMEM, VMEM, VMEM, VMEM],
        out_specs=(VMEM, VMEM),
        scratch_shapes=[pltpu.VMEM((HD, WIDE), wide)],
        compiler_params=room(8),
        name="late",
    )(table, kv, near_memory(dlogit), near_memory(out_t))
    summed = pl.pallas_call(
        add_kernel,
        out_shape=shaped((NODES * SHARE, HD), low),
        in_specs=[SMEM, VMEM],
        out_specs=HBM,
        scratch_shapes=[
            pltpu.VMEM(((NODES + 1) * SHARE, HD), wide),
            pltpu.VMEM(((NODES + 1) * SHARE, HD), wide),
            pltpu.VMEM((NODES * SHARE, HD), low),
            pltpu.SemaphoreType.DMA((4,)),
        ],
        compiler_params=room(8),
        name="add",
    )(table, near_memory(terms))
    back = lax.all_to_all(summed, everyone, split_axis=0, concat_axis=0, tiled=True)
    key_grad, value_grad = pl.pallas_call(
        finish_kernel,
        out_shape=(shaped((rows, KVH * HD), wide), shaped((rows, KVH * HD), wide)),
        in_specs=[VMEM],
        out_specs=(VMEM, VMEM),
        compiler_params=room(8),
        name="finish",
    )(near_memory(back))
    return (attended, query_grad, key_grad, value_grad)


def solution(mesh):
    mesh = Mesh(mesh.devices.reshape(FAR, NEAR, KVH), ("far", "near", "head"))
    leaf = ("far", "near")
    token = ("far", "near", "head")
    return jax.shard_map(
        per_device,
        mesh=mesh,
        in_specs=(P(leaf, "head"), P(token, None), P(token, None), P(leaf, "head"), P(), P()),
        out_specs=(P(leaf, "head"), P(leaf, "head"), P(token, None), P(token, None)),
        check_vma=False,
    )
```
